32 devices in a mesh: row: 8 (over z, x), col: 4 (over y, core).
Axes of the slice: x: 2, y: 2, z: 4, core: 2. Of those that a mesh axis runs over, the one named last changes fastest.
Arguments:
- tokens: bfloat16 [512, 4096], P('row', 'col'), may hold values from -6 to 6
- gate_weight: bfloat16 [4096, 14336], P('col', 'row'), may hold values from -0.09375 to 0.09375
- up_weight: bfloat16 [4096, 14336], P('col', 'row'), may hold values from -0.09375 to 0.09375
- down_weight: bfloat16 [14336, 4096], P('row', 'col'), may hold values from -0.046875 to 0.046875
- gate_mask: int32 [32, 112], replicated, may hold values 0 or 1
- up_mask: int32 [32, 112], replicated, may hold values 0 or 1
- down_mask: int32 [112, 32], replicated, may hold values 0 or 1
- out_grad: bfloat16 [512, 4096], P('row', 'col'), may hold values from -6 to 6
Outputs:
- mixed: bfloat16 [512, 4096], P('row', 'col')
- input_grad: bfloat16 [512, 4096], P('row', 'col')
- gate_grad: float32 [4096, 14336], P('col', 'row')
- up_grad: float32 [4096, 14336], P('col', 'row')
- down_grad: float32 [14336, 4096], P('row', 'col')
The draws below stay inside these ranges and needn't reach their ends.
All inputs are finite; a program needn't handle non-finite values.
Results may differ from the reference program's by a relative error of at most 0.0049.
Values may be sent and summed in bfloat16 or wider, within the bound.
No kernel may reach another device: no remote copies, remote signals or barrier semaphores. Data moves between devices by JAX's collectives and lax.ppermute only.
A program may use at most 128 MiB of HBM per device.

```python
import jax
import jax.numpy as jnp

D = 4096
FF = 14336
BLOCK = 128
TOKENS = 512


def set_ends(entries, rng, low, high):
    longest = entries.shape.index(max(entries.shape))
    spots = []
    for shift in (0, 1):
        where = [jax.random.randint(jax.random.fold_in(rng, axis), (), 0, length) for axis, length in enumerate(entries.shape)]
        where[longest] = (where[longest] + shift) % entries.shape[longest]
        spots.append(tuple(where))
    return entries.at[spots[0]].set(low).at[spots[1]].set(high)


def shard_levels(own_key, extent, split, low, high):
    factor_of = 1.0
    for axis_at, shards_of in split:
        draws = jax.random.uniform(jax.random.fold_in(jax.random.fold_in(own_key, 6), axis_at), (shards_of,), jnp.float32, low / len(split), high / len(split))
        factor_of = factor_of * jnp.repeat(jnp.exp(draws), extent[axis_at] // shards_of).reshape((-1,) + (1,) * (len(extent) - 1 - axis_at))
    return factor_of


def centred(stream_key, dims, width, bound, pieces=(), kind=jnp.bfloat16):
    level = shard_levels(stream_key, dims, pieces, -0.22, 0.18) if pieces else 1.0
    drawn = jax.random.normal(stream_key, dims, jnp.float32) * width * level
    return jnp.minimum(jnp.maximum(drawn, -bound), bound).astype(kind)


def setup_inputs(seed: int = 0) -> dict:
    arg_keys = jax.random.split(jax.random.key(seed), 9)
    return {
        "tokens": centred(arg_keys[0], (TOKENS, D), 1.0, 6.0, ((0, 8), (1, 4))),
        "gate_weight": centred(arg_keys[1], (D, FF), D ** -0.5, 0.09375, ((0, 4), (1, 8))),
        "up_weight": centred(arg_keys[2], (D, FF), D ** -0.5, 0.09375, ((0, 4), (1, 8))),
        "down_weight": centred(arg_keys[3], (FF, D), FF ** -0.5, 0.046875, ((0, 8), (1, 4))),
        "gate_mask": set_ends((jax.random.randint(arg_keys[4], (D // BLOCK, FF // BLOCK), 0, 8) < 5).astype(jnp.int32), jax.random.fold_in(arg_keys[4], 1), 0, 1),
        "up_mask": set_ends((jax.random.randint(arg_keys[5], (D // BLOCK, FF // BLOCK), 0, 8) < 5).astype(jnp.int32), jax.random.fold_in(arg_keys[5], 1), 0, 1),
        "down_mask": set_ends((jax.random.randint(arg_keys[6], (FF // BLOCK, D // BLOCK), 0, 8) < 5).astype(jnp.int32), jax.random.fold_in(arg_keys[6], 1), 0, 1),
        "out_grad": centred(arg_keys[7], (TOKENS, D), 1.0, 6.0, ((0, 8), (1, 4))),
    }


def expand(mask):
    return jnp.repeat(jnp.repeat(mask, BLOCK, axis=0), BLOCK, axis=1)


def reference(tokens, gate_weight, up_weight, down_weight, gate_mask, up_mask, down_mask, out_grad):
    keep_gate = expand(gate_mask)
    keep_up = expand(up_mask)
    keep_down = expand(down_mask)
    zero = jnp.zeros((), jnp.bfloat16)
    kept_gate = jnp.where(keep_gate > 0, gate_weight, zero)
    kept_up = jnp.where(keep_up > 0, up_weight, zero)
    kept_down = jnp.where(keep_down > 0, down_weight, zero)
    gate = jnp.dot(tokens, kept_gate, preferred_element_type=jnp.float32)
    up = jnp.dot(tokens, kept_up, preferred_element_type=jnp.float32)
    sig = jax.nn.sigmoid(gate)
    hidden = (gate * sig * up).astype(jnp.bfloat16)
    mixed = jnp.dot(hidden, kept_down, preferred_element_type=jnp.float32).astype(jnp.bfloat16)
    hidden_grad = jnp.dot(out_grad, kept_down.T, preferred_element_type=jnp.float32)
    dgate = (hidden_grad * up * sig * (1.0 + gate * (1.0 - sig))).astype(jnp.bfloat16)
    dup = (hidden_grad * gate * sig).astype(jnp.bfloat16)
    input_grad = (jnp.dot(dgate, kept_gate.T, preferred_element_type=jnp.float32)
                  + jnp.dot(dup, kept_up.T, preferred_element_type=jnp.float32)).astype(jnp.bfloat16)
    gate_grad = keep_gate.astype(jnp.float32) * jnp.dot(tokens.T, dgate, preferred_element_type=jnp.float32)
    up_grad = keep_up.astype(jnp.float32) * jnp.dot(tokens.T, dup, preferred_element_type=jnp.float32)
    down_grad = keep_down.astype(jnp.float32) * jnp.dot(hidden.T, out_grad, preferred_element_type=jnp.float32)
    return mixed, input_grad, gate_grad, up_grad, down_grad
```

```python
import functools

import jax
import jax.numpy as jnp
from jax import lax
from jax.experimental import pallas as pl
from jax.experimental.pallas import tpu as pltpu
from jax.sharding import PartitionSpec as P

BLOCK = 128
CORES = 2
BF16 = jnp.bfloat16
F32 = jnp.float32


def tile_of(units):
    return 256 if units % 256 == 0 else units


def expand(mask, unit_start, units):
    block = (unit_start + lax.broadcasted_iota(jnp.int32, (1, units), 1)) // BLOCK
    pick = (lax.broadcasted_iota(jnp.int32, (mask.shape[1], 1), 0) == block).astype(BF16)
    return jnp.dot(mask.astype(BF16), pick, preferred_element_type=F32)


def keep_rows(weight, mask):
    mask = mask.astype(weight.dtype)
    parts = [
        weight[k * BLOCK : (k + 1) * BLOCK] * mask[k : k + 1] for k in range(mask.shape[0])
    ]
    return jnp.concatenate(parts, axis=0)


def keep_columns(weight, mask):
    parts = []
    for k in range(mask.shape[1]):
        wide = jnp.broadcast_to(mask[:, k : k + 1], (mask.shape[0], BLOCK))
        parts.append(weight[:, k * BLOCK : (k + 1) * BLOCK] * wide.astype(weight.dtype))
    return jnp.concatenate(parts, axis=1)


def dot_nt(left, right):
    return lax.dot_general(
        left, right, (((1,), (1,)), ((), ())), preferred_element_type=F32
    )


def gather_lhs(shards, lhs):
    half = shards[0].shape[0] // 2
    own = half * len(shards)
    for k, shard in enumerate(shards):
        lhs[pl.ds(k * half, half), :] = shard[pl.ds(0, half), :]
        lhs[pl.ds(own + k * half, half), :] = shard[pl.ds(half, half), :]
    return own


def whole(shape):
    return pl.BlockSpec(shape, lambda j: (0,) * len(shape))


def cost(flops, *arrays):
    return pl.CostEstimate(
        flops=flops,
        bytes_accessed=sum(a.size * a.dtype.itemsize for a in arrays),
        transcendentals=0,
    )


def partial_gate_up(shards, gate_weight, up_weight, keep_gate, keep_up):
    n = len(shards)
    rows, feats = shards[0].shape
    own = n * rows // 2
    units = gate_weight.shape[1]
    tile = tile_of(units)

    def body(*refs):
        tokens = refs[:n]
        gate_ref, up_ref, kg_ref, ku_ref, keep_ref, send_ref, lhs = refs[n:]

        @pl.when(pl.program_id(0) == 0)
        def _():
            gather_lhs(tokens, lhs)

        for k, (weight, mask) in enumerate(((gate_ref, kg_ref), (up_ref, ku_ref))):
            out = jnp.dot(
                lhs[...], keep_rows(weight[...], mask[...]), preferred_element_type=F32
            )
            keep_ref[k] = out[:own]
            send_ref[k] = out[own:].astype(BF16)

    out_shape = (
        jax.ShapeDtypeStruct((2, own, units), F32),
        jax.ShapeDtypeStruct((2, own, units), BF16),
    )
    wide = pl.BlockSpec((feats, tile), lambda j: (0, j))
    narrow = pl.BlockSpec((keep_gate.shape[0], tile), lambda j: (0, j))
    return pl.pallas_call(
        body,
        grid=(units // tile,),
        in_specs=[whole((rows, feats))] * n + [wide, wide, narrow, narrow],
        out_specs=[pl.BlockSpec((2, own, tile), lambda j: (0, 0, j))] * 2,
        out_shape=out_shape,
        scratch_shapes=[pltpu.VMEM((2 * own, feats), BF16)],
        cost_estimate=cost(
            8 * own * feats * units, *shards, gate_weight, up_weight, *out_shape
        ),
        name="gate_up",
    )(*shards, gate_weight, up_weight, keep_gate, keep_up)


def partial_hidden_grad(shards, down_weight, keep_down):
    n = len(shards)
    rows, feats = shards[0].shape
    own = n * rows // 2
    units = down_weight.shape[0]
    tile = tile_of(units)

    def body(*refs):
        grads = refs[:n]
        down_ref, kd_ref, keep_ref, send_ref, lhs = refs[n:]

        @pl.when(pl.program_id(0) == 0)
        def _():
            gather_lhs(grads, lhs)

        out = dot_nt(lhs[...], keep_columns(down_ref[...], kd_ref[...]))
        keep_ref[...] = out[:own]
        send_ref[...] = out[own:].astype(BF16)

    out_shape = (
        jax.ShapeDtypeStruct((own, units), F32),
        jax.ShapeDtypeStruct((own, units), BF16),
    )
    return pl.pallas_call(
        body,
        grid=(units // tile,),
        in_specs=[whole((rows, feats))] * n
        + [
            pl.BlockSpec((tile, feats), lambda j: (j, 0)),
            pl.BlockSpec((tile, keep_down.shape[1]), lambda j: (j, 0)),
        ],
        out_specs=[pl.BlockSpec((own, tile), lambda j: (0, j))] * 2,
        out_shape=out_shape,
        scratch_shapes=[pltpu.VMEM((2 * own, feats), BF16)],
        cost_estimate=cost(4 * own * feats * units, *shards, down_weight, *out_shape),
        name="hidden_grad",
    )(*shards, down_weight, keep_down)


def store_shards(total, outs, half):
    own = half * len(outs)
    for k, out in enumerate(outs):
        out[pl.ds(0, half), :] = total[pl.ds(k * half, half), :].astype(out.dtype)
        out[pl.ds(half, half), :] = total[pl.ds(own + k * half, half), :].astype(out.dtype)


def partial_mixed(own_part, other_part, down_weight, keep_down, dtypes):
    n = len(dtypes)
    own, units = own_part.shape
    half = own // n
    feats = down_weight.shape[1]
    tile = tile_of(units)

    def body(*refs):
        own_ref, other_ref, down_ref, kd_ref = refs[:4]
        outs, total = refs[4 : 4 + n], refs[4 + n]
        step = pl.program_id(0)
        weight = keep_columns(down_ref[...], kd_ref[...])
        lhs = jnp.concatenate([own_ref[...], other_ref[...]], axis=0)
        out = jnp.dot(lhs, weight, preferred_element_type=F32)

        @pl.when(step == 0)
        def _():
            total[...] = out

        @pl.when(step > 0)
        def _():
            total[...] += out

        @pl.when(step == pl.num_programs(0) - 1)
        def _():
            store_shards(total, outs, half)

    out_shape = [jax.ShapeDtypeStruct((2 * half, feats), d) for d in dtypes]
    part = pl.BlockSpec((own, tile), lambda j: (0, j))
    return pl.pallas_call(
        body,
        grid=(units // tile,),
        in_specs=[
            part,
            part,
            pl.BlockSpec((tile, feats), lambda j: (j, 0)),
            pl.BlockSpec((tile, keep_down.shape[1]), lambda j: (j, 0)),
        ],
        out_specs=[whole((2 * half, feats))] * n,
        out_shape=out_shape,
        scratch_shapes=[pltpu.VMEM((2 * own, feats), F32)],
        cost_estimate=cost(
            4 * own * feats * units, own_part, other_part, down_weight, *out_shape
        ),
        name="mixed",
    )(own_part, other_part, down_weight, keep_down)


def partial_input_grad(own_part, other_part, gate_weight, up_weight, keep_gate, keep_up, dtypes):
    n = len(dtypes)
    _, own, units = own_part.shape
    half = own // n
    feats = gate_weight.shape[0]
    tile = tile_of(units)

    def body(*refs):
        own_ref, other_ref, gate_ref, up_ref, kg_ref, ku_ref = refs[:6]
        outs, total = refs[6 : 6 + n], refs[6 + n]
        step = pl.program_id(0)
        out = None
        for k, (weight, mask) in enumerate(((gate_ref, kg_ref), (up_ref, ku_ref))):
            lhs = jnp.concatenate([own_ref[k], other_ref[k]], axis=0)
            term = dot_nt(lhs, keep_rows(weight[...], mask[...]))
            out = term if out is None else out + term

        @pl.when(step == 0)
        def _():
            total[...] = out

        @pl.when(step > 0)
        def _():
            total[...] += out

        @pl.when(step == pl.num_programs(0) - 1)
        def _():
            store_shards(total, outs, half)

    out_shape = [jax.ShapeDtypeStruct((2 * half, feats), d) for d in dtypes]
    part = pl.BlockSpec((2, own, tile), lambda j: (0, 0, j))
    wide = pl.BlockSpec((feats, tile), lambda j: (0, j))
    narrow = pl.BlockSpec((keep_gate.shape[0], tile), lambda j: (0, j))
    return pl.pallas_call(
        body,
        grid=(units // tile,),
        in_specs=[part, part, wide, wide, narrow, narrow],
        out_specs=[whole((2 * half, feats))] * n,
        out_shape=out_shape,
        scratch_shapes=[pltpu.VMEM((2 * own, feats), F32)],
        cost_estimate=cost(
            8 * own * feats * units, own_part, other_part, gate_weight, up_weight, *out_shape
        ),
        name="input_grad",
    )(own_part, other_part, gate_weight, up_weight, keep_gate, keep_up)


def stack_tokens(groups, lhs):
    at = 0
    for shards in groups:
        half = shards[0].shape[0] // 2
        for start in (0, half):
            for shard in shards:
                lhs[pl.ds(at, half), :] = shard[pl.ds(start, half), :]
                at += half


def grad_gate_up(groups, parts, keep_gate, keep_up):
    sizes = [len(g) for g in groups]
    flat = [s for g in groups for s in g]
    pieces = [a for pair in parts for a in pair]
    n = len(flat)
    rows, feats = flat[0].shape
    units = pieces[0].shape[2]
    tile = tile_of(units)
    tokens = n * rows

    def body(*refs):
        shards = list(refs[:n])
        part_refs = refs[n : n + len(pieces)]
        kg_ref, ku_ref, dg_ref, du_ref, lhs, turned = refs[n + len(pieces) :]

        @pl.when(pl.program_id(0) == 0)
        def _():
            nested = []
            at = 0
            for size in sizes:
                nested.append(shards[at : at + size])
                at += size
            stack_tokens(nested, lhs)
            turned[...] = lhs[...].T

        for k, (mask, out_ref) in enumerate(((kg_ref, dg_ref), (ku_ref, du_ref))):
            right = jnp.concatenate([p[k] for p in part_refs], axis=0)
            out = jnp.dot(turned[...], right, preferred_element_type=F32)
            for b in range(mask.shape[0]):
                out_ref[pl.ds(b * BLOCK, BLOCK), :] = (
                    out[b * BLOCK : (b + 1) * BLOCK] * mask[pl.ds(b, 1), :]
                )

    out_shape = [jax.ShapeDtypeStruct((feats, units), F32)] * 2
    narrow = pl.BlockSpec((keep_gate.shape[0], tile), lambda j: (0, j))
    return pl.pallas_call(
        body,
        grid=(units // tile,),
        in_specs=[whole((rows, feats))] * n
        + [pl.BlockSpec((2, p.shape[1], tile), lambda j: (0, 0, j)) for p in pieces]
        + [narrow, narrow],
        out_specs=[pl.BlockSpec((feats, tile), lambda j: (0, j))] * 2,
        out_shape=out_shape,
        scratch_shapes=[
            pltpu.VMEM((tokens, feats), BF16),
            pltpu.VMEM((feats, tokens), BF16),
        ],
        cost_estimate=cost(4 * tokens * feats * units, *flat, *pieces, *out_shape),
        name="grad_gate_up",
    )(*flat, *pieces, keep_gate, keep_up)


def grad_down(groups, parts, keep_down):
    sizes = [len(g) for g in groups]
    flat = [s for g in groups for s in g]
    pieces = [a for pair in parts for a in pair]
    n = len(flat)
    rows, feats = flat[0].shape
    units = pieces[0].shape[1]
    tile = tile_of(units)
    tokens = n * rows

    def body(*refs):
        shards = list(refs[:n])
        part_refs = refs[n : n + len(pieces)]
        kd_ref, out_ref, rhs = refs[n + len(pieces) :]

        @pl.when(pl.program_id(0) == 0)
        def _():
            nested = []
            at = 0
            for size in sizes:
                nested.append(shards[at : at + size])
                at += size
            stack_tokens(nested, rhs)

        left = jnp.concatenate([p[...] for p in part_refs], axis=0)
        out = lax.dot_general(
            left, rhs[...], (((0,), (0,)), ((), ())), preferred_element_type=F32
        )
        out_ref[...] = keep_columns(out, kd_ref[...])

    out_shape = jax.ShapeDtypeStruct((units, feats), F32)
    return pl.pallas_call(
        body,
        grid=(units // tile,),
        in_specs=[whole((rows, feats))] * n
        + [pl.BlockSpec((p.shape[0], tile), lambda j: (0, j)) for p in pieces]
        + [pl.BlockSpec((tile, keep_down.shape[1]), lambda j: (j, 0))],
        out_specs=pl.BlockSpec((tile, feats), lambda j: (j, 0)),
        out_shape=out_shape,
        scratch_shapes=[pltpu.VMEM((tokens, feats), BF16)],
        cost_estimate=cost(2 * tokens * feats * units, *flat, *pieces, out_shape),
        name="grad_down",
    )(*flat, *pieces, keep_down)


def after(value, *others):
    return lax.optimization_barrier((value, *others))[0]


def per_device(
    rows_n,
    cols_n,
    tokens,
    gate_weight,
    up_weight,
    down_weight,
    gate_mask,
    up_mask,
    down_mask,
    out_grad,
):
    cores = CORES if cols_n % CORES == 0 else 1
    ys = cols_n // cores
    xs = 1
    while (2 * xs) ** 2 <= rows_n and rows_n % (2 * xs) == 0:
        xs *= 2
    zs = rows_n // xs
    feats, units = gate_weight.shape
    blocks = feats // BLOCK
    row_index = lax.axis_index("row")
    col_index = lax.axis_index("col")
    core = col_index % cores
    half = tokens.shape[0] // 2

    def shift_z(value, by):
        pairs = [(i, ((i // xs + by) % zs) * xs + i % xs) for i in range(rows_n)]
        return lax.ppermute(value, "row", pairs)

    def shift_x(value, by):
        pairs = [(i, i // xs * xs + (i % xs + by) % xs) for i in range(rows_n)]
        return lax.ppermute(value, "row", pairs)

    def shift_y(value, by):
        pairs = [(i, (i // cores + by) % ys * cores + i % cores) for i in range(cols_n)]
        return lax.ppermute(value, "col", pairs)

    def swap_core(value):
        pairs = [(i, i // cores * cores + (i % cores + 1) % cores) for i in range(cols_n)]
        return lax.ppermute(value, "col", pairs)

    def turn(value):
        return jnp.where(core == 1, jnp.roll(value, half, axis=0), value)

    unit_start = row_index * units
    keep = [
        expand(
            lax.dynamic_slice(m, (col_index * blocks, 0), (blocks, m.shape[1])),
            unit_start,
            units,
        )
        for m in (gate_mask, up_mask, down_mask.T)
    ]
    keep_gate, keep_up, keep_down = keep[0], keep[1], keep[2].T

    order = [0] + [d for k in range(1, zs // 2 + 1) for d in dict.fromkeys((k, zs - k))]
    tok, grad = {}, {}
    for held, own in ((tok, turn(tokens)), (grad, turn(out_grad))):
        if held is grad:
            own = after(own, tok[order[1], 0]) if zs > 1 else own
        held[0, 0] = turn_own = own
        for dx in range(1, xs):
            held[0, dx] = shift_x(turn_own, dx)
        for dz in order[1:]:
            held[dz, 0] = shift_z(turn_own, dz)
        for dz in order[1:]:
            for dx in range(1, xs):
                held[dz, dx] = shift_x(held[dz, 0], dx)
    first = [(0, 0)]
    second = [(0, dx) for dx in range(1, xs)]
    rest = [[(dz, dx) for dx in range(xs)] for dz in order[1:]]
    chunks = [first, second, *rest]
    chunks = [c for c in chunks if c]

    def exchange(keep_part, send_part):
        near = keep_part + swap_core(send_part)
        out = near.astype(BF16)
        far = [shift_y(out, by) for by in range(1, ys)]
        for value in far:
            near = near + value
        return near

    both = {}
    hidden_grad = {}
    for k, chunk in enumerate(chunks):
        both[k] = exchange(
            *partial_gate_up(
                [tok[s] for s in chunk], gate_weight, up_weight, keep_gate, keep_up
            )
        )
        if k == 0:
            hidden_grad[k] = exchange(
                *partial_hidden_grad([grad[s] for s in chunk], down_weight, keep_down)
            )
    back = [*range(2, len(chunks)), 1]
    for k in back:
        hidden_grad[k] = exchange(
            *partial_hidden_grad([grad[s] for s in chunks[k]], down_weight, keep_down)
        )

    hidden, pre = {}, {}
    mixed, inputs = {}, {}
    for k, chunk in enumerate(chunks):
        gate, up = both[k][0], both[k][1]
        sig = jax.nn.sigmoid(gate)
        own = (gate * sig * up).astype(BF16)
        hidden[k] = (own, swap_core(own))
        outs = partial_mixed(
            *hidden[k], down_weight, keep_down, [F32 if s[1] == 0 else BF16 for s in chunk]
        )
        mixed.update(zip(chunk, outs))
    for k in [0, *back]:
        chunk = chunks[k]
        gate, up = both[k][0], both[k][1]
        sig = jax.nn.sigmoid(gate)
        dgate = hidden_grad[k] * up * sig * (1.0 + gate * (1.0 - sig))
        dup = hidden_grad[k] * gate * sig
        own = jnp.stack([dgate.astype(BF16), dup.astype(BF16)])
        pre[k] = (own, swap_core(own))
        outs = partial_input_grad(
            *pre[k],
            gate_weight,
            up_weight,
            keep_gate,
            keep_up,
            [F32 if s[1] == 0 else BF16 for s in chunk],
        )
        inputs.update(zip(chunk, outs))

    def scatter(part):
        total = None
        for dz in [*order[1:], 0]:
            value = part[dz, 0]
            for dx in range(1, xs):
                value = value + shift_x(part[dz, dx], -dx)
            if dz:
                value = shift_z(value.astype(BF16), -dz).astype(F32)
            total = value if total is None else total + value
        return turn(total.astype(BF16))

    down_grad = grad_down(
        [[grad[s] for s in c] for c in chunks], [hidden[k] for k in range(len(chunks))], keep_down
    )
    gate_grad, up_grad = grad_gate_up(
        [[tok[s] for s in c] for c in chunks],
        [pre[k] for k in range(len(chunks))],
        keep_gate,
        keep_up,
    )
    return (scatter(mixed), scatter(inputs), gate_grad, up_grad, down_grad)


def solution(mesh):
    return jax.shard_map(
        functools.partial(per_device, mesh.shape["row"], mesh.shape["col"]),
        mesh=mesh,
        in_specs=(
            P("row", "col"),
            P("col", "row"),
            P("col", "row"),
            P("row", "col"),
            P(),
            P(),
            P(),
            P("row", "col"),
        ),
        out_specs=(
            P("row", "col"),
            P("row", "col"),
            P("col", "row"),
            P("col", "row"),
            P("row", "col"),
        ),
        check_vma=False,
    )
```

```python
import jax
import jax.numpy as jnp
from jax import lax
from jax.experimental import pallas as pl
from jax.experimental.pallas import tpu as pltpu
from jax.sharding import PartitionSpec as P

BLOCK = 128
CORES = 2
BF16 = jnp.bfloat16
F32 = jnp.float32
MIB = 1 << 20
PARTIALS_MIB = 24
PRODUCTS_MIB = 24
HBM = pl.BlockSpec(memory_space=pltpu.HBM)
VMEM = pl.BlockSpec(memory_space=pltpu.VMEM)


def tile_of(units):
    return 256 if units % 256 == 0 else units


def keep_rows(weight, mask):
    mask = mask.astype(weight.dtype)
    parts = [
        weight[k * BLOCK : (k + 1) * BLOCK] * mask[k : k + 1] for k in range(mask.shape[0])
    ]
    return jnp.concatenate(parts, axis=0)


def keep_columns(weight, mask):
    parts = []
    for k in range(mask.shape[1]):
        wide = jnp.broadcast_to(mask[:, k : k + 1], (mask.shape[0], BLOCK))
        parts.append(weight[:, k * BLOCK : (k + 1) * BLOCK] * wide.astype(weight.dtype))
    return jnp.concatenate(parts, axis=1)


def dot_nn(left, right):
    return jnp.dot(left, right, preferred_element_type=F32)


def dot_nt(left, right):
    return lax.dot_general(
        left, right, (((1,), (1,)), ((), ())), preferred_element_type=F32
    )


def dot_tn(left, right):
    return lax.dot_general(
        left, right, (((0,), (0,)), ((), ())), preferred_element_type=F32
    )


def cost(flops, *arrays):
    return pl.CostEstimate(
        flops=flops,
        bytes_accessed=sum(a.size * a.dtype.itemsize for a in arrays),
        transcendentals=0,
    )


def params(mib):
    return pltpu.CompilerParams(vmem_limit_bytes=mib * MIB)


def tiles(units):
    tile = tile_of(units)
    return tile, units // tile, lambda j: pl.ds(pl.multiple_of(j * tile, tile), tile)


def for_steps(steps, body):
    if steps == 1:
        body(0)
    else:
        lax.fori_loop(0, steps, lambda j, c: (body(j), c)[1], 0)


def prepare(where, tokens, out_grad, gate_mask, up_mask, down_mask, units):
    rows, feats = tokens.shape
    half = rows // 2
    blocks = feats // BLOCK
    sources = (gate_mask, up_mask, down_mask, tokens, out_grad)

    def body(where_ref, *refs):
        srcs, (pair, kg, ku, kd), bufs, sems = refs[:5], refs[5:9], refs[9:14], refs[14]
        copies = [
            pltpu.make_async_copy(src, buf, sems.at[k])
            for k, (src, buf) in enumerate(zip(srcs, bufs))
        ]
        for copy in copies:
            copy.start()
        col, row, core = where_ref[0], where_ref[1], where_ref[2]
        count = gate_mask.shape[1]
        block = lax.div(
            row * units + lax.broadcasted_iota(jnp.int32, (count, units), 1), BLOCK
        )
        pick = (lax.broadcasted_iota(jnp.int32, (count, units), 0) == block).astype(F32)
        pick = pick.astype(BF16)
        shape = (blocks, gate_mask.shape[0])
        feature = col * blocks + lax.broadcasted_iota(jnp.int32, shape, 0)
        mine = (lax.broadcasted_iota(jnp.int32, shape, 1) == feature).astype(F32).astype(BF16)
        for k, out in enumerate((kg, ku, kd)):
            copies[k].wait()
            mask = dot_nn(mine, bufs[k][...].astype(F32).astype(BF16))
            if k < 2:
                out[...] = dot_nn(mask.astype(BF16), pick)
            else:
                out[...] = dot_tn(pick, mask.T.astype(BF16))
        for k in range(2):
            copies[3 + k].wait()
            low, high = bufs[3 + k][pl.ds(0, half), :], bufs[3 + k][pl.ds(half, half), :]
            pair[k, pl.ds(0, half), :] = jnp.where(core == 1, high, low)
            pair[k, pl.ds(half, half), :] = jnp.where(core == 1, low, high)

    return pl.pallas_call(
        body,
        in_specs=[pl.BlockSpec(memory_space=pltpu.SMEM)] + [HBM] * 5,
        out_specs=[VMEM] * 4,
        out_shape=[
            jax.ShapeDtypeStruct((2, rows, feats), BF16),
            jax.ShapeDtypeStruct((blocks, units), F32),
            jax.ShapeDtypeStruct((blocks, units), F32),
            jax.ShapeDtypeStruct((units, blocks), F32),
        ],
        scratch_shapes=[pltpu.VMEM(a.shape, a.dtype) for a in sources]
        + [pltpu.SemaphoreType.DMA((5,))],
        cost_estimate=pl.CostEstimate(flops=0, bytes_accessed=4 * MIB, transcendentals=0),
        compiler_params=params(16),
        name="prepare",
    )(where, *sources)


def partials(shards, weights, keeps=None):
    n = len(shards)
    m = 3 if keeps else 0
    _, rows, feats = shards[0].shape
    half = rows // 2
    own = n * half
    units = weights[0].shape[1]
    _, steps, at = tiles(units)

    def body(*refs):
        pairs = refs[:n]
        w_refs = refs[n : n + 3]
        masks = refs[n + 3 : n + 3 + m]
        keep_ref, send_ref = refs[n + 3 + m : n + 5 + m]
        bufs = refs[n + 5 + m : n + 5 + 2 * m] if keeps else w_refs
        lhs = refs[n + 5 + 2 * m]

        def copies(j):
            part = at(j)
            spots = [(slice(None), part), (slice(None), part), (part, slice(None))]
            return [
                pltpu.make_async_copy(src.at[spot], dst.at[spot], refs[-1].at[k, j])
                for k, (src, dst, spot) in enumerate(zip(w_refs, bufs, spots))
            ]

        def start(j):
            for copy in copies(j):
                copy.start()

        if keeps:
            for_steps(steps, start)
        for k in range(2):
            for i, pair in enumerate(pairs):
                lhs[k, pl.ds(i * half, half), :] = pair[k, pl.ds(0, half), :]
                lhs[k, pl.ds(own + i * half, half), :] = pair[k, pl.ds(half, half), :]

        def step(j):
            part = at(j)
            gate, up, down = (
                (lambda k=k: bufs[k][:, part] if k < 2 else bufs[k][part, :]) for k in range(3)
            )
            if keeps:
                for copy in copies(j):
                    copy.wait()
                bufs[0][:, part] = keep_rows(gate(), masks[0][:, part])
                bufs[1][:, part] = keep_rows(up(), masks[1][:, part])
                bufs[2][part, :] = keep_columns(down(), masks[2][part, :])
            outs = (dot_nn(lhs[0], gate()), dot_nn(lhs[0], up()), dot_nt(lhs[1], down()))
            for k, out in enumerate(outs):
                keep_ref[k, :, part] = out[:own]
                send_ref[k, :, part] = out[own:]

        for_steps(steps, step)

    out_shape = [jax.ShapeDtypeStruct((3, own, units), F32)] * 2
    if keeps:
        out_shape += [jax.ShapeDtypeStruct(w.shape, w.dtype) for w in weights]
    scratch = [pltpu.VMEM((2, 2 * own, feats), BF16)]
    if keeps:
        scratch.append(pltpu.SemaphoreType.DMA((3, steps)))
    return pl.pallas_call(
        body,
        in_specs=[VMEM] * n + [HBM if keeps else VMEM] * 3 + [VMEM] * m,
        out_specs=[VMEM] * (2 + m),
        out_shape=out_shape,
        scratch_shapes=scratch,
        cost_estimate=cost(12 * own * feats * units, *shards, *weights, *out_shape),
        compiler_params=params(PARTIALS_MIB),
        name="partials",
    )(*shards, *weights, *(keeps or ()))


def activate(keep, near, far):
    def body(*refs):
        keep_ref, near_ref = refs[:2]
        far_refs, out_ref = refs[2:-1], refs[-1]

        def total(k):
            value = keep_ref[k] + near_ref[k]
            for ref in far_refs:
                value = value + ref[k].astype(F32)
            return value

        gate, up, hidden_grad = total(0), total(1), total(2)
        sig = jax.nn.sigmoid(gate)
        act = gate * sig
        out_ref[0] = (act * up).astype(BF16)
        out_ref[1] = (hidden_grad * up * sig * (1.0 + gate * (1.0 - sig))).astype(BF16)
        out_ref[2] = (hidden_grad * act).astype(BF16)

    n = 3 + len(far)
    return pl.pallas_call(
        body,
        in_specs=[VMEM] * (n - 1),
        out_specs=VMEM,
        out_shape=jax.ShapeDtypeStruct(keep.shape, BF16),
        cost_estimate=cost(20 * keep.size, keep, near, *far),
        compiler_params=params(16),
        name="activate",
    )(keep, near, *far)


def products(parts, counts, slots, sizes, weights):
    pieces = [a for pair in parts for a in pair]
    n = len(pieces)
    units = pieces[0].shape[2]
    feats = weights[0].shape[0]
    half = pieces[0].shape[1] // counts[0]
    tokens = sum(p.shape[1] for p in pieces)
    _, steps, at = tiles(feats)
    outs_n = len(sizes)

    def body(*refs):
        piece_refs = refs[:n]
        gate_ref, up_ref, down_ref = refs[n : n + 3]
        outs, lhs = refs[n + 3 : n + 3 + outs_n], refs[n + 3 + outs_n]
        row = 0
        for piece in piece_refs:
            lhs[:, pl.ds(row, piece.shape[1]), :] = piece[...]
            row += piece.shape[1]

        def step(j):
            part = at(j)
            sums = (
                dot_nn(lhs[0], down_ref[:, part]),
                dot_nt(lhs[1], gate_ref[part, :]) + dot_nt(lhs[2], up_ref[part, :]),
            )
            row, shard = 0, 0
            for count in counts:
                for side in range(2):
                    for i in range(count):
                        out, place = slots[shard + i]
                        for k in range(2):
                            outs[out][place, k, pl.ds(side * half, half), part] = sums[k][
                                row : row + half
                            ].astype(outs[out].dtype)
                        row += half
                shard += count

        for_steps(steps, step)

    out_shape = [
        jax.ShapeDtypeStruct((size, 2, 2 * half, feats), BF16 if k else F32)
        for k, size in enumerate(sizes)
    ]
    return pl.pallas_call(
        body,
        in_specs=[VMEM] * (n + 3),
        out_specs=[VMEM] * outs_n,
        out_shape=out_shape,
        scratch_shapes=[pltpu.VMEM((3, tokens, units), BF16)],
        cost_estimate=cost(6 * tokens * feats * units, *pieces, *weights, *out_shape),
        compiler_params=params(PRODUCTS_MIB),
        name="products",
    )(*pieces, *weights)


def weight_grads(groups, parts, keeps):
    flat = [s for g in groups for s in g]
    pieces = [a for pair in parts for a in pair]
    n, m = len(flat), len(pieces)
    _, rows, feats = flat[0].shape
    half = rows // 2
    units = pieces[0].shape[2]
    tokens = n * rows
    tile, steps, at = tiles(units)

    def body(*refs):
        shards = list(refs[:n])
        piece_refs = refs[n : n + m]
        kg, ku, kd = refs[n + m : n + m + 3]
        grads = refs[n + m + 3 : n + m + 6]
        lhs, turned, rhs, gate_buf, up_buf, down_buf, sems = refs[n + m + 6 :]
        row, shard = 0, 0
        for group in groups:
            for side in range(2):
                for i in range(len(group)):
                    pair = shards[shard + i]
                    lhs[pl.ds(row, half), :] = pair[0, pl.ds(side * half, half), :]
                    rhs[pl.ds(row, half), :] = pair[1, pl.ds(side * half, half), :]
                    row += half
            shard += len(group)
        turned[...] = lhs[...].T

        def copies(j):
            part = at(j)
            return [
                pltpu.make_async_copy(src.at[j], dst, sems.at[k, j])
                for k, (src, dst) in enumerate(
                    (
                        (gate_buf, grads[0].at[:, part]),
                        (up_buf, grads[1].at[:, part]),
                        (down_buf, grads[2].at[part, :]),
                    )
                )
            ]

        def step(j):
            part = at(j)
            pre = [
                jnp.concatenate([p[k, :, part] for p in piece_refs], axis=0) for k in range(3)
            ]
            for buf, right, mask in ((gate_buf, pre[1], kg), (up_buf, pre[2], ku)):
                buf[j] = keep_rows(dot_nn(turned[...], right), mask[:, part])
            down_buf[j] = keep_columns(dot_tn(pre[0], rhs[...]), kd[part, :])
            for copy in copies(j):
                copy.start()

        def finish(j):
            for copy in copies(j):
                copy.wait()

        for_steps(steps, step)
        for_steps(steps, finish)

    out_shape = [
        jax.ShapeDtypeStruct((feats, units), F32),
        jax.ShapeDtypeStruct((feats, units), F32),
        jax.ShapeDtypeStruct((units, feats), F32),
    ]
    return pl.pallas_call(
        body,
        in_specs=[VMEM] * (n + m + 3),
        out_specs=[HBM] * 3,
        out_shape=out_shape,
        scratch_shapes=[
            pltpu.VMEM((tokens, feats), BF16),
            pltpu.VMEM((feats, tokens), BF16),
            pltpu.VMEM((tokens, feats), BF16),
            pltpu.VMEM((steps, feats, tile), F32),
            pltpu.VMEM((steps, feats, tile), F32),
            pltpu.VMEM((steps, tile, feats), F32),
            pltpu.SemaphoreType.DMA((3, steps)),
        ],
        cost_estimate=cost(6 * tokens * feats * units, *flat, *pieces, *out_shape),
        compiler_params=params(48),
        name="weight_grads",
    )(*flat, *pieces, *keeps)


def per_device(
    rows_n,
    cols_n,
    tokens,
    gate_weight,
    up_weight,
    down_weight,
    gate_mask,
    up_mask,
    down_mask,
    out_grad,
):
    cores = CORES if cols_n % CORES == 0 else 1
    ys = cols_n // cores
    xs = 1
    while (2 * xs) ** 2 <= rows_n and rows_n % (2 * xs) == 0:
        xs *= 2
    zs = rows_n // xs
    units = gate_weight.shape[1]
    row_index = lax.axis_index("row")
    col_index = lax.axis_index("col")
    core = col_index % cores
    half = tokens.shape[0] // 2

    def shift_z(value, by):
        pairs = [(i, ((i // xs + by) % zs) * xs + i % xs) for i in range(rows_n)]
        return lax.ppermute(value, "row", pairs)

    def shift_x(value, by):
        pairs = [(i, i // xs * xs + (i % xs + by) % xs) for i in range(rows_n)]
        return lax.ppermute(value, "row", pairs)

    def shift_y(value, by):
        pairs = [(i, (i // cores + by) % ys * cores + i % cores) for i in range(cols_n)]
        return lax.ppermute(value, "col", pairs)

    def swap_core(value):
        pairs = [(i, i // cores * cores + (i % cores + 1) % cores) for i in range(cols_n)]
        return lax.ppermute(value, "col", pairs)

    pair, *keeps = prepare(
        jnp.stack([col_index, row_index, core]),
        tokens,
        out_grad,
        gate_mask,
        up_mask,
        down_mask.T,
        units,
    )

    far_z = [d for k in range(1, zs // 2 + 1) for d in dict.fromkeys((k, zs - k))]
    held = {(0, 0): pair}
    for dz in far_z:
        held[dz, 0] = shift_z(pair, dz)
    for dx in range(1, xs):
        held[0, dx] = shift_x(pair, dx)
    for dz in far_z:
        for dx in range(1, xs):
            held[dz, dx] = shift_x(held[dz, 0], dx)

    z_groups = [far_z[k : k + 2] for k in range(0, len(far_z), 2)]
    chunks, groups = [[(0, 0)]], []
    for k, group in enumerate(z_groups):
        at = len(chunks)
        if k == 0:
            chunks.append([(dz, 0) for dz in group])
            chunks.append([(dz, dx) for dz in group for dx in range(1, xs)])
        else:
            chunks.append([(dz, dx) for dx in range(xs) for dz in group])
        groups.append([c for c in range(at, len(chunks)) if chunks[c]])
    chunks.append([(0, dx) for dx in range(1, xs)])
    groups.append([c for c in (0, len(chunks) - 1) if chunks[c]])

    parts = {}
    weights = (gate_weight, up_weight, down_weight)
    for k, chunk in enumerate(chunks):
        if not chunk:
            continue
        keep, send, *kept = partials([held[s] for s in chunk], weights, keeps if k == 0 else None)
        weights = kept or weights
        near = swap_core(send)
        out = (keep + near).astype(BF16)
        far = [shift_y(out, by) for by in range(1, ys)]
        own = activate(keep, near, far)
        parts[k] = (own, swap_core(own))

    total = None
    for group in groups:
        shards = [s for c in group for s in chunks[c]]
        dzs = list(dict.fromkeys(s[0] for s in shards))
        outs = products(
            [parts[c] for c in group],
            [len(chunks[c]) for c in group],
            [(dx, dzs.index(dz)) for dz, dx in shards],
            [len(dzs)] * xs,
            weights,
        )
        sums = outs[0]
        for dx in range(1, xs):
            sums = sums + shift_x(outs[dx], -dx)
        for k, dz in enumerate(dzs):
            value = sums[k]
            if dz:
                value = shift_z(value.astype(BF16), -dz)
            total = value.astype(F32) if total is None else total + value
    order = [k for k in range(len(chunks)) if chunks[k]]
    grads = weight_grads(
        [[held[s] for s in chunks[k]] for k in order], [parts[k] for k in order], keeps
    )
    total = total.astype(BF16)
    total = jnp.where(core == 1, jnp.roll(total, half, axis=1), total)
    return (total[0], total[1], *grads)


def solution(mesh):
    def whole(*args):
        return per_device(mesh.shape["row"], mesh.shape["col"], *args)

    return jax.shard_map(
        whole,
        mesh=mesh,
        in_specs=(
            P("row", "col"),
            P("col", "row"),
            P("col", "row"),
            P("row", "col"),
            P(),
            P(),
            P(),
            P("row", "col"),
        ),
        out_specs=(
            P("row", "col"),
            P("row", "col"),
            P("col", "row"),
            P("col", "row"),
            P("row", "col"),
        ),
        check_vma=False,
    )
```

```python
import jax
import jax.numpy as jnp
from jax import lax
from jax.experimental import pallas as pl
from jax.experimental.pallas import tpu as pltpu
from jax.sharding import PartitionSpec as P

BLOCK = 128
CORES = 2
BF16 = jnp.bfloat16
F32 = jnp.float32
MIB = 1 << 20
FIRST_MIB = 39
PARTIALS_MIB = 8
PRODUCTS_MIB = 10
HBM = pl.BlockSpec(memory_space=pltpu.HBM)
VMEM = pl.BlockSpec(memory_space=pltpu.VMEM)
SMEM = pl.BlockSpec(memory_space=pltpu.SMEM)


def tile_of(units):
    return 256 if units % 256 == 0 else units


def keep_rows(weight, mask):
    mask = mask.astype(weight.dtype)
    parts = [
        weight[k * BLOCK : (k + 1) * BLOCK] * mask[k : k + 1] for k in range(mask.shape[0])
    ]
    return jnp.concatenate(parts, axis=0)


def keep_columns(weight, mask):
    parts = []
    for k in range(mask.shape[1]):
        wide = jnp.broadcast_to(mask[:, k : k + 1], (mask.shape[0], BLOCK))
        parts.append(weight[:, k * BLOCK : (k + 1) * BLOCK] * wide.astype(weight.dtype))
    return jnp.concatenate(parts, axis=1)


def dot_nn(left, right):
    return jnp.dot(left, right, preferred_element_type=F32)


def dot_nt(left, right):
    return lax.dot_general(
        left, right, (((1,), (1,)), ((), ())), preferred_element_type=F32
    )


def dot_tn(left, right):
    return lax.dot_general(
        left, right, (((0,), (0,)), ((), ())), preferred_element_type=F32
    )


def cost(flops, *arrays):
    return pl.CostEstimate(
        flops=flops,
        bytes_accessed=sum(a.size * a.dtype.itemsize for a in arrays),
        transcendentals=0,
    )


def params(mib):
    return pltpu.CompilerParams(vmem_limit_bytes=mib * MIB)


def tiles(units):
    tile = tile_of(units)
    return tile, units // tile, lambda j: pl.ds(pl.multiple_of(j * tile, tile), tile)


def for_steps(steps, body):
    if steps == 1:
        body(0)
    else:
        lax.fori_loop(0, steps, lambda j, c: (body(j), c)[1], 0)


def load_half(pair, k, half, core, second):
    first = pl.multiple_of(half * (1 - core if second else core), half)
    return pair[k, pl.ds(first, half), :]


def first_partials(where, shard, weights, masks):
    _, rows, feats = shard.shape
    half = rows // 2
    units = weights[0].shape[1]
    blocks = feats // BLOCK
    _, steps, at = tiles(units)

    def body(where_ref, pair, masks_ref, *refs):
        w_refs, (keep_ref, send_ref), bufs = refs[:3], refs[3:5], refs[5:8]
        expanded, lhs, sems = refs[8:11], refs[11], refs[12]
        col, row, core = where_ref[0], where_ref[1], where_ref[2]

        def copies(j):
            part = at(j)
            spots = [(slice(None), part), (slice(None), part), (part, slice(None))]
            return [
                pltpu.make_async_copy(src.at[spot], dst.at[spot], sems.at[k, j])
                for k, (src, dst, spot) in enumerate(zip(w_refs, bufs, spots))
            ]

        def start(j):
            for copy in copies(j):
                copy.start()

        for_steps(steps, start)
        count = masks_ref.shape[1]
        block = lax.div(
            row * units + lax.broadcasted_iota(jnp.int32, (count, units), 1), BLOCK
        )
        pick = (lax.broadcasted_iota(jnp.int32, (count, units), 0) == block).astype(F32)
        pick = pick.astype(BF16)
        total = masks_ref.shape[0] // 3
        feature = col * blocks + lax.broadcasted_iota(jnp.int32, (blocks, total), 0)
        mine = (
            (lax.broadcasted_iota(jnp.int32, (blocks, total), 1) == feature)
            .astype(F32)
            .astype(BF16)
        )
        for k, out in enumerate(expanded):
            mask = dot_nn(mine, masks_ref[pl.ds(k * total, total), :])
            if k < 2:
                out[...] = dot_nn(mask.astype(BF16), pick)
            else:
                out[...] = dot_tn(pick, mask.T.astype(BF16))
        for k in range(2):
            for second in range(2):
                lhs[k, pl.ds(second * half, half), :] = load_half(pair, k, half, core, second)

        def step(j):
            part = at(j)
            for copy in copies(j):
                copy.wait()
            gate = keep_rows(bufs[0][:, part], expanded[0][:, part])
            up = keep_rows(bufs[1][:, part], expanded[1][:, part])
            down = keep_columns(bufs[2][part, :], expanded[2][part, :])
            bufs[0][:, part] = gate
            bufs[1][:, part] = up
            bufs[2][part, :] = down
            for k, out in enumerate((dot_nn(lhs[0], gate), dot_nn(lhs[0], up), dot_nt(lhs[1], down))):
                keep_ref[k, :, part] = out[:half]
                send_ref[k, :, part] = out[half:]

        for_steps(steps, step)

    out_shape = [jax.ShapeDtypeStruct((3, half, units), F32)] * 2
    out_shape += [jax.ShapeDtypeStruct(w.shape, w.dtype) for w in weights]
    out_shape += [jax.ShapeDtypeStruct((blocks, units), F32)] * 2
    out_shape.append(jax.ShapeDtypeStruct((units, blocks), F32))
    return pl.pallas_call(
        body,
        in_specs=[SMEM, VMEM, VMEM] + [HBM] * 3,
        out_specs=[VMEM] * 8,
        out_shape=out_shape,
        scratch_shapes=[
            pltpu.VMEM((2, rows, feats), BF16),
            pltpu.SemaphoreType.DMA((3, steps)),
        ],
        cost_estimate=cost(12 * half * feats * units, shard, *weights, *out_shape),
        compiler_params=params(FIRST_MIB),
        name="first_partials",
    )(where, shard, masks, *weights)


def partials(where, shards, weights):
    n = len(shards)
    _, rows, feats = shards[0].shape
    half = rows // 2
    own = n * half
    units = weights[0].shape[1]
    _, steps, at = tiles(units)

    def body(where_ref, *refs):
        pairs = refs[:n]
        gate_ref, up_ref, down_ref, keep_ref, send_ref, lhs = refs[n:]
        core = where_ref[2]
        for k in range(2):
            for i, pair in enumerate(pairs):
                for second in range(2):
                    lhs[k, pl.ds(second * own + i * half, half), :] = load_half(
                        pair, k, half, core, second
                    )

        def step(j):
            part = at(j)
            outs = (
                dot_nn(lhs[0], gate_ref[:, part]),
                dot_nn(lhs[0], up_ref[:, part]),
                dot_nt(lhs[1], down_ref[part, :]),
            )
            for k, out in enumerate(outs):
                keep_ref[k, :, part] = out[:own]
                send_ref[k, :, part] = out[own:]

        for_steps(steps, step)

    out_shape = [jax.ShapeDtypeStruct((3, own, units), F32)] * 2
    return pl.pallas_call(
        body,
        in_specs=[SMEM] + [VMEM] * (n + 3),
        out_specs=[VMEM] * 2,
        out_shape=out_shape,
        scratch_shapes=[pltpu.VMEM((2, 2 * own, feats), BF16)],
        cost_estimate=cost(12 * own * feats * units, *shards, *weights, *out_shape),
        compiler_params=params(PARTIALS_MIB),
        name="partials",
    )(where, *shards, *weights)


def finish(where, parts):
    _, rows, feats = parts[0].shape
    half = rows // 2

    def body(where_ref, *refs):
        part_refs, outs = refs[:-2], refs[-2:]
        core = where_ref[2]
        for k, out in enumerate(outs):
            total = part_refs[0][k].astype(F32)
            for ref in part_refs[1:]:
                total = total + ref[k].astype(F32)
            total = total.astype(BF16)
            low, high = total[:half], total[half:]
            out[pl.ds(0, half), :] = jnp.where(core == 1, high, low)
            out[pl.ds(half, half), :] = jnp.where(core == 1, low, high)

    out_shape = [jax.ShapeDtypeStruct((rows, feats), BF16)] * 2
    return pl.pallas_call(
        body,
        in_specs=[SMEM] + [VMEM] * len(parts),
        out_specs=[VMEM] * 2,
        out_shape=out_shape,
        cost_estimate=cost(2 * rows * feats * len(parts), *parts, *out_shape),
        compiler_params=params(8),
        name="finish",
    )(where, *parts)


def activate(keep, near, far):
    def body(*refs):
        keep_ref, near_ref = refs[:2]
        far_refs, out_ref = refs[2:-1], refs[-1]

        def total(k):
            value = keep_ref[k] + near_ref[k]
            for ref in far_refs:
                value = value + ref[k].astype(F32)
            return value

        gate, up, hidden_grad = total(0), total(1), total(2)
        sig = jax.nn.sigmoid(gate)
        act = gate * sig
        out_ref[0] = (act * up).astype(BF16)
        out_ref[1] = (hidden_grad * up * sig * (1.0 + gate * (1.0 - sig))).astype(BF16)
        out_ref[2] = (hidden_grad * act).astype(BF16)

    n = 3 + len(far)
    return pl.pallas_call(
        body,
        in_specs=[VMEM] * (n - 1),
        out_specs=VMEM,
        out_shape=jax.ShapeDtypeStruct(keep.shape, BF16),
        cost_estimate=cost(20 * keep.size, keep, near, *far),
        compiler_params=params(8),
        name="activate",
    )(keep, near, *far)


def products(parts, counts, slots, sizes, weights):
    pieces = [a for pair in parts for a in pair]
    n = len(pieces)
    units = pieces[0].shape[2]
    feats = weights[0].shape[0]
    half = pieces[0].shape[1] // counts[0]
    tokens = sum(p.shape[1] for p in pieces)
    _, steps, at = tiles(feats)
    outs_n = len(sizes)

    def body(*refs):
        piece_refs = refs[:n]
        gate_ref, up_ref, down_ref = refs[n : n + 3]
        outs, lhs = refs[n + 3 : n + 3 + outs_n], refs[n + 3 + outs_n]
        row = 0
        for piece in piece_refs:
            lhs[:, pl.ds(row, piece.shape[1]), :] = piece[...]
            row += piece.shape[1]

        def step(j):
            part = at(j)
            sums = (
                dot_nn(lhs[0], down_ref[:, part]),
                dot_nt(lhs[1], gate_ref[part, :]) + dot_nt(lhs[2], up_ref[part, :]),
            )
            row, shard = 0, 0
            for count in counts:
                for side in range(2):
                    for i in range(count):
                        out, place = slots[shard + i]
                        for k in range(2):
                            outs[out][place, k, pl.ds(side * half, half), part] = sums[k][
                                row : row + half
                            ].astype(outs[out].dtype)
                        row += half
                shard += count

        for_steps(steps, step)

    out_shape = [
        jax.ShapeDtypeStruct((size, 2, 2 * half, feats), BF16 if k else F32)
        for k, size in enumerate(sizes)
    ]
    return pl.pallas_call(
        body,
        in_specs=[VMEM] * (n + 3),
        out_specs=[VMEM] * outs_n,
        out_shape=out_shape,
        scratch_shapes=[pltpu.VMEM((3, tokens, units), BF16)],
        cost_estimate=cost(6 * tokens * feats * units, *pieces, *weights, *out_shape),
        compiler_params=params(PRODUCTS_MIB),
        name="products",
    )(*pieces, *weights)


def weight_grads(where, groups, parts, keeps):
    flat = [s for g in groups for s in g]
    pieces = [a for pair in parts for a in pair]
    n, m = len(flat), len(pieces)
    _, rows, feats = flat[0].shape
    half = rows // 2
    units = pieces[0].shape[2]
    tokens = n * rows
    tile, steps, at = tiles(units)

    def body(where_ref, *refs):
        shards = list(refs[:n])
        core = where_ref[2]
        piece_refs = refs[n : n + m]
        kg, ku, kd = refs[n + m : n + m + 3]
        grads = refs[n + m + 3 : n + m + 6]
        lhs, turned, rhs, gate_buf, up_buf, down_buf, sems = refs[n + m + 6 :]
        row, shard = 0, 0
        for group in groups:
            for side in range(2):
                for i in range(len(group)):
                    pair = shards[shard + i]
                    lhs[pl.ds(row, half), :] = load_half(pair, 0, half, core, side)
                    rhs[pl.ds(row, half), :] = load_half(pair, 1, half, core, side)
                    row += half
            shard += len(group)
        turned[...] = lhs[...].T

        def copies(j):
            part = at(j)
            return [
                pltpu.make_async_copy(src.at[j], dst, sems.at[k, j])
                for k, (src, dst) in enumerate(
                    (
                        (gate_buf, grads[0].at[:, part]),
                        (up_buf, grads[1].at[:, part]),
                        (down_buf, grads[2].at[part, :]),
                    )
                )
            ]

        def step(j):
            part = at(j)
            pre = [
                jnp.concatenate([p[k, :, part] for p in piece_refs], axis=0) for k in range(3)
            ]
            for buf, right, mask in ((gate_buf, pre[1], kg), (up_buf, pre[2], ku)):
                buf[j] = keep_rows(dot_nn(turned[...], right), mask[:, part])
            down_buf[j] = keep_columns(dot_tn(pre[0], rhs[...]), kd[part, :])
            for copy in copies(j):
                copy.start()

        def finish(j):
            for copy in copies(j):
                copy.wait()

        for_steps(steps, step)
        for_steps(steps, finish)

    out_shape = [
        jax.ShapeDtypeStruct((feats, units), F32),
        jax.ShapeDtypeStruct((feats, units), F32),
        jax.ShapeDtypeStruct((units, feats), F32),
    ]
    return pl.pallas_call(
        body,
        in_specs=[SMEM] + [VMEM] * (n + m + 3),
        out_specs=[HBM] * 3,
        out_shape=out_shape,
        scratch_shapes=[
            pltpu.VMEM((tokens, feats), BF16),
            pltpu.VMEM((feats, tokens), BF16),
            pltpu.VMEM((tokens, feats), BF16),
            pltpu.VMEM((steps, feats, tile), F32),
            pltpu.VMEM((steps, feats, tile), F32),
            pltpu.VMEM((steps, tile, feats), F32),
            pltpu.SemaphoreType.DMA((3, steps)),
        ],
        cost_estimate=cost(6 * tokens * feats * units, *flat, *pieces, *out_shape),
        compiler_params=params(32),
        name="weight_grads",
    )(where, *flat, *pieces, *keeps)


def per_device(
    rows_n,
    cols_n,
    tokens,
    gate_weight,
    up_weight,
    down_weight,
    gate_mask,
    up_mask,
    down_mask,
    out_grad,
):
    cores = CORES if cols_n % CORES == 0 else 1
    ys = cols_n // cores
    xs = 1
    while (2 * xs) ** 2 <= rows_n and rows_n % (2 * xs) == 0:
        xs *= 2
    zs = rows_n // xs
    row_index = lax.axis_index("row")
    col_index = lax.axis_index("col")
    core = col_index % cores

    def shift_z(value, by):
        pairs = [(i, ((i // xs + by) % zs) * xs + i % xs) for i in range(rows_n)]
        return lax.ppermute(value, "row", pairs)

    def shift_x(value, by):
        pairs = [(i, i // xs * xs + (i % xs + by) % xs) for i in range(rows_n)]
        return lax.ppermute(value, "row", pairs)

    def shift_y(value, by):
        pairs = [(i, (i // cores + by) % ys * cores + i % cores) for i in range(cols_n)]
        return lax.ppermute(value, "col", pairs)

    def swap_core(value):
        pairs = [(i, i // cores * cores + (i % cores + 1) % cores) for i in range(cols_n)]
        return lax.ppermute(value, "col", pairs)

    where = jnp.stack([col_index, row_index, core])
    pair = jnp.stack([tokens, out_grad])
    masks = jnp.concatenate([gate_mask, up_mask, down_mask.T]).astype(BF16)

    far_z = [d for k in range(1, zs // 2 + 1) for d in dict.fromkeys((k, zs - k))]
    held = {(0, 0): pair}
    for dz in far_z:
        held[dz, 0] = shift_z(pair, dz)
    for dx in range(1, xs):
        held[0, dx] = shift_x(pair, dx)
    for dz in far_z:
        for dx in range(1, xs):
            held[dz, dx] = shift_x(held[dz, 0], dx)

    z_groups = [far_z[k : k + 2] for k in range(0, len(far_z), 2)]
    chunks, groups = [[(0, 0)]], []
    for k, group in enumerate(z_groups):
        at = len(chunks)
        if k == 0:
            chunks.append([(dz, 0) for dz in group])
            chunks.append([(dz, dx) for dz in group for dx in range(1, xs)])
        else:
            chunks.append([(dz, dx) for dx in range(xs) for dz in group])
        groups.append([c for c in range(at, len(chunks)) if chunks[c]])
    chunks.append([(0, dx) for dx in range(1, xs)])
    groups.append([c for c in (0, len(chunks) - 1) if chunks[c]])

    parts = {}
    weights = (gate_weight, up_weight, down_weight)
    for k, chunk in enumerate(chunks):
        if not chunk:
            continue
        at = "last" if k == len(chunks) - 1 else k
        shards = [held[s] for s in chunk]
        if k == 0:
            keep, send, *rest = first_partials(where, *shards, weights, masks)
            weights, keeps = rest[:3], rest[3:]
        else:
            keep, send = partials(where, shards, weights)
        near = swap_core(send)
        out = (keep + near).astype(BF16)
        far = [shift_y(out, by) for by in range(1, ys)]
        own = activate(keep, near, far)
        parts[k] = (own, swap_core(own))

    terms = []
    for group in groups:
        shards = [s for c in group for s in chunks[c]]
        dzs = list(dict.fromkeys(s[0] for s in shards))
        outs = products(
            [parts[c] for c in group],
            [len(chunks[c]) for c in group],
            [(dx, dzs.index(dz)) for dz, dx in shards],
            [len(dzs)] * xs,
            weights,
        )
        sums = outs[0]
        for dx in range(1, xs):
            sums = sums + shift_x(outs[dx], -dx)
        for k, dz in enumerate(dzs):
            value = sums[k]
            if dz:
                value = shift_z(value.astype(BF16), -dz)
            terms.append(value)
    order = [k for k in range(len(chunks)) if chunks[k]]
    grads = weight_grads(
        where, [[held[s] for s in chunks[k]] for k in order], [parts[k] for k in order], keeps
    )
    return (*finish(where, terms), *grads)


def solution(mesh):
    def whole(*args):
        return per_device(mesh.shape["row"], mesh.shape["col"], *args)

    return jax.shard_map(
        whole,
        mesh=mesh,
        in_specs=(
            P("row", "col"),
            P("col", "row"),
            P("col", "row"),
            P("row", "col"),
            P(),
            P(),
            P(),
            P("row", "col"),
        ),
        out_specs=(
            P("row", "col"),
            P("row", "col"),
            P("col", "row"),
            P("col", "row"),
            P("row", "col"),
        ),
        check_vma=False,
    )
```

```python
import jax
import jax.numpy as jnp
from jax import lax
from jax.experimental import pallas as pl
from jax.experimental.pallas import tpu as pltpu
from jax.sharding import PartitionSpec as P

BLOCK = 128
CORES = 2
BF16 = jnp.bfloat16
F32 = jnp.float32
MIB = 1 << 20
FIRST_MIB = 39
PARTIALS_MIB = 8
PRODUCTS_MIB = 10
HBM = pl.BlockSpec(memory_space=pltpu.HBM)
VMEM = pl.BlockSpec(memory_space=pltpu.VMEM)
SMEM = pl.BlockSpec(memory_space=pltpu.SMEM)


def tile_of(units):
    return 256 if units % 256 == 0 else units


def keep_rows(weight, mask):
    mask = mask.astype(weight.dtype)
    parts = [
        weight[k * BLOCK : (k + 1) * BLOCK] * mask[k : k + 1] for k in range(mask.shape[0])
    ]
    return jnp.concatenate(parts, axis=0)


def keep_columns(weight, mask):
    parts = []
    for k in range(mask.shape[1]):
        wide = jnp.broadcast_to(mask[:, k : k + 1], (mask.shape[0], BLOCK))
        parts.append(weight[:, k * BLOCK : (k + 1) * BLOCK] * wide.astype(weight.dtype))
    return jnp.concatenate(parts, axis=1)


def dot_nn(left, right):
    return jnp.dot(left, right, preferred_element_type=F32)


def dot_nt(left, right):
    return lax.dot_general(
        left, right, (((1,), (1,)), ((), ())), preferred_element_type=F32
    )


def dot_tn(left, right):
    return lax.dot_general(
        left, right, (((0,), (0,)), ((), ())), preferred_element_type=F32
    )


def cost(flops, *arrays):
    return pl.CostEstimate(
        flops=flops,
        bytes_accessed=sum(a.size * a.dtype.itemsize for a in arrays),
        transcendentals=0,
    )


def params(mib):
    return pltpu.CompilerParams(vmem_limit_bytes=mib * MIB)


def tiles(units):
    tile = tile_of(units)
    return tile, units // tile, lambda j: pl.ds(pl.multiple_of(j * tile, tile), tile)


def for_steps(steps, body, unroll=False):
    if steps == 1:
        body(0)
    else:
        lax.fori_loop(0, steps, lambda j, c: (body(j), c)[1], 0, unroll=unroll)


def split_halves(core, store):
    for c in range(CORES):

        @pl.when(core == c)
        def _():
            for second in range(2):
                store(second, (c + second) % 2)


def first_partials(where, shard, weights, masks):
    _, rows, feats = shard.shape
    half = rows // 2
    units = weights[0].shape[1]
    blocks = feats // BLOCK
    _, steps, at = tiles(units)

    def body(where_ref, pair, masks_ref, *refs):
        w_refs, (keep_ref, send_ref), bufs = refs[:3], refs[3:5], refs[5:8]
        expanded, lhs, sems = refs[8:11], refs[11], refs[12]
        col, row, core = where_ref[0], where_ref[1], where_ref[2]

        def copies(j):
            part = at(j)
            spots = [(slice(None), part), (slice(None), part), (part, slice(None))]
            return [
                pltpu.make_async_copy(src.at[spot], dst.at[spot], sems.at[k, j])
                for k, (src, dst, spot) in enumerate(zip(w_refs, bufs, spots))
            ]

        def start(j):
            for copy in copies(j):
                copy.start()

        for_steps(steps, start)
        count = masks_ref.shape[1]
        block = lax.div(
            row * units + lax.broadcasted_iota(jnp.int32, (count, units), 1), BLOCK
        )
        pick = (lax.broadcasted_iota(jnp.int32, (count, units), 0) == block).astype(F32)
        pick = pick.astype(BF16)
        total = masks_ref.shape[0] // 3
        feature = col * blocks + lax.broadcasted_iota(jnp.int32, (blocks, total), 0)
        mine = (
            (lax.broadcasted_iota(jnp.int32, (blocks, total), 1) == feature)
            .astype(F32)
            .astype(BF16)
        )
        for k, out in enumerate(expanded):
            mask = masks_ref[pl.ds(k * total, total), :].astype(F32).astype(BF16)
            mask = dot_nn(mine, mask)
            if k < 2:
                out[...] = dot_nn(mask.astype(BF16), pick)
            else:
                out[...] = dot_tn(pick, mask.T.astype(BF16))

        def store(second, side):
            lhs[:, pl.ds(second * half, half), :] = pair[:, pl.ds(side * half, half), :]

        split_halves(core, store)

        def step(j):
            part = at(j)
            for copy in copies(j):
                copy.wait()
            gate = keep_rows(bufs[0][:, part], expanded[0][:, part])
            up = keep_rows(bufs[1][:, part], expanded[1][:, part])
            down = keep_columns(bufs[2][part, :], expanded[2][part, :])
            bufs[0][:, part] = gate
            bufs[1][:, part] = up
            bufs[2][part, :] = down
            for k, out in enumerate((dot_nn(lhs[0], gate), dot_nn(lhs[0], up), dot_nt(lhs[1], down))):
                keep_ref[k, :, part] = out[:half]
                send_ref[k, :, part] = out[half:]

        for_steps(steps, step)

    out_shape = [jax.ShapeDtypeStruct((3, half, units), F32)] * 2
    out_shape += [jax.ShapeDtypeStruct(w.shape, w.dtype) for w in weights]
    out_shape += [jax.ShapeDtypeStruct((blocks, units), F32)] * 2
    out_shape.append(jax.ShapeDtypeStruct((units, blocks), F32))
    return pl.pallas_call(
        body,
        in_specs=[SMEM, VMEM, VMEM] + [HBM] * 3,
        out_specs=[VMEM] * 8,
        out_shape=out_shape,
        scratch_shapes=[
            pltpu.VMEM((2, rows, feats), BF16),
            pltpu.SemaphoreType.DMA((3, steps)),
        ],
        cost_estimate=cost(12 * half * feats * units, shard, *weights, *out_shape),
        compiler_params=params(FIRST_MIB),
        name="first_partials",
    )(where, shard, masks, *weights)


def partials(where, shards, weights):
    n = len(shards)
    _, rows, feats = shards[0].shape
    half = rows // 2
    own = n * half
    units = weights[0].shape[1]
    _, steps, at = tiles(units)

    def body(where_ref, *refs):
        pairs = refs[:n]
        gate_ref, up_ref, down_ref, keep_ref, send_ref, lhs = refs[n:]
        core = where_ref[2]

        def store(second, side):
            for i, pair in enumerate(pairs):
                lhs[:, pl.ds(second * own + i * half, half), :] = pair[
                    :, pl.ds(side * half, half), :
                ]

        split_halves(core, store)

        def step(j):
            part = at(j)
            outs = (
                dot_nn(lhs[0], gate_ref[:, part]),
                dot_nn(lhs[0], up_ref[:, part]),
                dot_nt(lhs[1], down_ref[part, :]),
            )
            for k, out in enumerate(outs):
                keep_ref[k, :, part] = out[:own]
                send_ref[k, :, part] = out[own:]

        for_steps(steps, step, True)

    out_shape = [jax.ShapeDtypeStruct((3, own, units), F32)] * 2
    return pl.pallas_call(
        body,
        in_specs=[SMEM] + [VMEM] * (n + 3),
        out_specs=[VMEM] * 2,
        out_shape=out_shape,
        scratch_shapes=[pltpu.VMEM((2, 2 * own, feats), BF16)],
        cost_estimate=cost(12 * own * feats * units, *shards, *weights, *out_shape),
        compiler_params=params(PARTIALS_MIB),
        name="partials",
    )(where, *shards, *weights)


def finish(where, parts):
    _, rows, feats = parts[0].shape
    half = rows // 2

    def body(where_ref, *refs):
        part_refs, outs = refs[:-2], refs[-2:]
        core = where_ref[2]
        for k, out in enumerate(outs):
            total = part_refs[0][k].astype(F32)
            for ref in part_refs[1:]:
                total = total + ref[k].astype(F32)
            total = total.astype(BF16)
            low, high = total[:half], total[half:]
            out[pl.ds(0, half), :] = jnp.where(core == 1, high, low)
            out[pl.ds(half, half), :] = jnp.where(core == 1, low, high)

    out_shape = [jax.ShapeDtypeStruct((rows, feats), BF16)] * 2
    return pl.pallas_call(
        body,
        in_specs=[SMEM] + [VMEM] * len(parts),
        out_specs=[VMEM] * 2,
        out_shape=out_shape,
        cost_estimate=cost(2 * rows * feats * len(parts), *parts, *out_shape),
        compiler_params=params(8),
        name="finish",
    )(where, *parts)


def activate(keep, near, far):
    def body(*refs):
        keep_ref, near_ref = refs[:2]
        far_refs, out_ref = refs[2:-1], refs[-1]

        def total(k):
            value = keep_ref[k] + near_ref[k]
            for ref in far_refs:
                value = value + ref[k].astype(F32)
            return value

        gate, up, hidden_grad = total(0), total(1), total(2)
        sig = jax.nn.sigmoid(gate)
        act = gate * sig
        out_ref[0] = (act * up).astype(BF16)
        out_ref[1] = (hidden_grad * up * sig * (1.0 + gate * (1.0 - sig))).astype(BF16)
        out_ref[2] = (hidden_grad * act).astype(BF16)

    n = 3 + len(far)
    return pl.pallas_call(
        body,
        in_specs=[VMEM] * (n - 1),
        out_specs=VMEM,
        out_shape=jax.ShapeDtypeStruct(keep.shape, BF16),
        cost_estimate=cost(20 * keep.size, keep, near, *far),
        compiler_params=params(8),
        name="activate",
    )(keep, near, *far)


def products(shards, slots, sizes, weights):
    pieces, spots = [], []
    for own, other, place, half in shards:
        for piece in (own, other):
            known = [k for k, p in enumerate(pieces) if p is piece]
            if not known:
                pieces.append(piece)
            spots.append((known[0] if known else len(pieces) - 1, place * half))
    n = len(pieces)
    units = pieces[0].shape[2]
    feats = weights[0].shape[0]
    tokens = 2 * half * len(shards)
    _, steps, at = tiles(feats)
    outs_n = len(sizes)

    def body(*refs):
        gate_ref, up_ref, down_ref = refs[n : n + 3]
        outs, lhs = refs[n + 3 : n + 3 + outs_n], refs[n + 3 + outs_n]
        for k, (piece, row) in enumerate(spots):
            lhs[:, pl.ds(k * half, half), :] = refs[piece][:, pl.ds(row, half), :]

        def step(j):
            part = at(j)
            sums = (
                dot_nn(lhs[0], down_ref[:, part]),
                dot_nt(lhs[1], gate_ref[part, :]) + dot_nt(lhs[2], up_ref[part, :]),
            )
            for i, (out, place) in enumerate(slots):
                for k in range(2):
                    outs[out][place, k, :, part] = sums[k][
                        2 * half * i : 2 * half * (i + 1)
                    ].astype(outs[out].dtype)

        for_steps(steps, step, True)

    out_shape = [
        jax.ShapeDtypeStruct((size, 2, 2 * half, feats), BF16 if k else F32)
        for k, size in enumerate(sizes)
    ]
    return pl.pallas_call(
        body,
        in_specs=[VMEM] * (n + 3),
        out_specs=[VMEM] * outs_n,
        out_shape=out_shape,
        scratch_shapes=[pltpu.VMEM((3, tokens, units), BF16)],
        cost_estimate=cost(6 * tokens * feats * units, *pieces, *weights, *out_shape),
        compiler_params=params(PRODUCTS_MIB),
        name="products",
    )(*pieces, *weights)


def weight_grads(where, groups, parts, keeps):
    flat = [s for g in groups for s in g]
    pieces = [a for pair in parts for a in pair]
    n, m = len(flat), len(pieces)
    _, rows, feats = flat[0].shape
    half = rows // 2
    units = pieces[0].shape[2]
    tokens = n * rows
    tile, steps, at = tiles(units)

    def body(where_ref, *refs):
        shards = list(refs[:n])
        core = where_ref[2]
        piece_refs = refs[n : n + m]
        kg, ku, kd = refs[n + m : n + m + 3]
        grads = refs[n + m + 3 : n + m + 6]
        lhs, turned, rhs, gate_buf, up_buf, down_buf, sems = refs[n + m + 6 :]

        def store(second, side):
            row, shard = 0, 0
            for group in groups:
                size = len(group) * half
                for i in range(len(group)):
                    at_row = pl.ds(row + second * size + i * half, half)
                    lhs[at_row, :] = shards[shard + i][0, pl.ds(side * half, half), :]
                    rhs[at_row, :] = shards[shard + i][1, pl.ds(side * half, half), :]
                row += 2 * size
                shard += len(group)

        split_halves(core, store)
        turned[...] = lhs[...].T

        def copies(j):
            part = at(j)
            return [
                pltpu.make_async_copy(src.at[j], dst, sems.at[k, j])
                for k, (src, dst) in enumerate(
                    (
                        (gate_buf, grads[0].at[:, part]),
                        (up_buf, grads[1].at[:, part]),
                        (down_buf, grads[2].at[part, :]),
                    )
                )
            ]

        def step(j):
            part = at(j)
            pre = [
                jnp.concatenate([p[k, :, part] for p in piece_refs], axis=0) for k in range(3)
            ]
            for buf, right, mask in ((gate_buf, pre[1], kg), (up_buf, pre[2], ku)):
                buf[j] = keep_rows(dot_nn(turned[...], right), mask[:, part])
            down_buf[j] = keep_columns(dot_tn(pre[0], rhs[...]), kd[part, :])
            for copy in copies(j):
                copy.start()

        def finish(j):
            for copy in copies(j):
                copy.wait()

        for_steps(steps, step)
        for_steps(steps, finish)

    out_shape = [
        jax.ShapeDtypeStruct((feats, units), F32),
        jax.ShapeDtypeStruct((feats, units), F32),
        jax.ShapeDtypeStruct((units, feats), F32),
    ]
    return pl.pallas_call(
        body,
        in_specs=[SMEM] + [VMEM] * (n + m + 3),
        out_specs=[HBM] * 3,
        out_shape=out_shape,
        scratch_shapes=[
            pltpu.VMEM((tokens, feats), BF16),
            pltpu.VMEM((feats, tokens), BF16),
            pltpu.VMEM((tokens, feats), BF16),
            pltpu.VMEM((steps, feats, tile), F32),
            pltpu.VMEM((steps, feats, tile), F32),
            pltpu.VMEM((steps, tile, feats), F32),
            pltpu.SemaphoreType.DMA((3, steps)),
        ],
        cost_estimate=cost(6 * tokens * feats * units, *flat, *pieces, *out_shape),
        compiler_params=params(32),
        name="weight_grads",
    )(where, *flat, *pieces, *keeps)


def per_device(
    rows_n,
    cols_n,
    tokens,
    gate_weight,
    up_weight,
    down_weight,
    gate_mask,
    up_mask,
    down_mask,
    out_grad,
):
    cores = CORES if cols_n % CORES == 0 else 1
    ys = cols_n // cores
    xs = 1
    while (2 * xs) ** 2 <= rows_n and rows_n % (2 * xs) == 0:
        xs *= 2
    zs = rows_n // xs
    row_index = lax.axis_index("row")
    col_index = lax.axis_index("col")
    core = col_index % cores

    def shift_z(value, by):
        pairs = [(i, ((i // xs + by) % zs) * xs + i % xs) for i in range(rows_n)]
        return lax.ppermute(value, "row", pairs)

    def shift_x(value, by):
        pairs = [(i, i // xs * xs + (i % xs + by) % xs) for i in range(rows_n)]
        return lax.ppermute(value, "row", pairs)

    def shift_y(value, by):
        pairs = [(i, (i // cores + by) % ys * cores + i % cores) for i in range(cols_n)]
        return lax.ppermute(value, "col", pairs)

    def swap_core(value):
        pairs = [(i, i // cores * cores + (i % cores + 1) % cores) for i in range(cols_n)]
        return lax.ppermute(value, "col", pairs)

    where = jnp.stack([col_index, row_index, core])
    pair = jnp.stack([tokens, out_grad])
    masks = jnp.concatenate([gate_mask, up_mask, down_mask.T])

    far_z = [d for k in range(1, zs // 2 + 1) for d in dict.fromkeys((k, zs - k))]
    held = {(0, 0): pair}
    for dz in far_z:
        held[dz, 0] = shift_z(pair, dz)
    for dx in range(1, xs):
        held[0, dx] = shift_x(pair, dx)
    for dz in far_z:
        for dx in range(1, xs):
            held[dz, dx] = shift_x(held[dz, 0], dx)

    far_x = range(1, xs)
    near_z = far_z[:2]
    chunks = {"own": [(0, 0)], "a": [(dz, 0) for dz in near_z]}
    chunks["b"] = [(dz, dx) for dz in near_z[:1] for dx in far_x]
    for k in range(2, len(far_z), 2):
        chunks[f"m{k}"] = [(dz, dx) for dx in range(xs) for dz in far_z[k : k + 2]]
    chunks["c"] = [(dz, dx) for dz in near_z[1:] for dx in far_x]
    chunks["x"] = [(0, dx) for dx in far_x]
    groups = {"b": near_z[:1]}
    for k in range(2, len(far_z), 2):
        groups[f"m{k}"] = far_z[k : k + 2]
    groups["c"] = near_z[1:]
    groups["x"] = [0]
    chunks = {name: chunk for name, chunk in chunks.items() if chunk}
    groups = {name: group for name, group in groups.items() if group}

    parts = {}
    weights = (gate_weight, up_weight, down_weight)
    for name, chunk in chunks.items():
        shards = [held[s] for s in chunk]
        if name == "own":
            keep, send, *rest = first_partials(where, *shards, weights, masks)
            weights, keeps = rest[:3], rest[3:]
        else:
            keep, send = partials(where, shards, weights)
        near = swap_core(send)
        out = (keep + near).astype(BF16)
        far = [shift_y(out, by) for by in range(1, ys)]
        own = activate(keep, near, far)
        parts[name] = (own, swap_core(own))

    half = tokens.shape[0] // 2
    homes = {
        s: (*parts[name], k, half) for name, chunk in chunks.items() for k, s in enumerate(chunk)
    }
    terms = []
    for group in groups.values():
        shards = [(dz, dx) for dx in range(xs) for dz in group]
        outs = products(
            [homes[s] for s in shards],
            [(dx, group.index(dz)) for dz, dx in shards],
            [len(group)] * xs,
            weights,
        )
        sums = outs[0]
        for dx in far_x:
            sums = sums + shift_x(outs[dx], -dx)
        for k, dz in enumerate(group):
            value = sums[k]
            if dz:
                value = shift_z(value.astype(BF16), -dz)
            terms.append(value)
    grads = weight_grads(
        where,
        [[held[s] for s in chunk] for chunk in chunks.values()],
        [parts[name] for name in chunks],
        keeps,
    )
    return (*finish(where, terms[::-1]), *grads)


def solution(mesh):
    def whole(*args):
        return per_device(mesh.shape["row"], mesh.shape["col"], *args)

    return jax.shard_map(
        whole,
        mesh=mesh,
        in_specs=(
            P("row", "col"),
            P("col", "row"),
            P("col", "row"),
            P("row", "col"),
            P(),
            P(),
            P(),
            P("row", "col"),
        ),
        out_specs=(
            P("row", "col"),
            P("row", "col"),
            P("col", "row"),
            P("col", "row"),
            P("row", "col"),
        ),
        check_vma=False,
    )
```

```python
import jax
import jax.numpy as jnp
from jax import lax
from jax.experimental import pallas as pl
from jax.experimental.pallas import tpu as pltpu
from jax.sharding import PartitionSpec as P

BLOCK = 128
CORES = 2
BF16 = jnp.bfloat16
F32 = jnp.float32
MIB = 1 << 20
FIRST_MIB = 39
PARTIALS_MIB = 8
PRODUCTS_MIB = 10
HBM = pl.BlockSpec(memory_space=pltpu.HBM)
VMEM = pl.BlockSpec(memory_space=pltpu.VMEM)
SMEM = pl.BlockSpec(memory_space=pltpu.SMEM)


def tile_of(units):
    return 256 if units % 256 == 0 else units


def keep_rows(weight, mask):
    mask = mask.astype(weight.dtype)
    parts = [
        weight[k * BLOCK : (k + 1) * BLOCK] * mask[k : k + 1] for k in range(mask.shape[0])
    ]
    return jnp.concatenate(parts, axis=0)


def keep_columns(weight, mask):
    parts = []
    for k in range(mask.shape[1]):
        wide = jnp.broadcast_to(mask[:, k : k + 1], (mask.shape[0], BLOCK))
        parts.append(weight[:, k * BLOCK : (k + 1) * BLOCK] * wide.astype(weight.dtype))
    return jnp.concatenate(parts, axis=1)


def dot_nn(left, right):
    return jnp.dot(left, right, preferred_element_type=F32)


def dot_nt(left, right):
    return lax.dot_general(
        left, right, (((1,), (1,)), ((), ())), preferred_element_type=F32
    )


def dot_tn(left, right):
    return lax.dot_general(
        left, right, (((0,), (0,)), ((), ())), preferred_element_type=F32
    )


def cost(flops, *arrays):
    return pl.CostEstimate(
        flops=flops,
        bytes_accessed=sum(a.size * a.dtype.itemsize for a in arrays),
        transcendentals=0,
    )


def params(mib):
    return pltpu.CompilerParams(vmem_limit_bytes=mib * MIB)


def tiles(units):
    tile = tile_of(units)
    return tile, units // tile, lambda j: pl.ds(pl.multiple_of(j * tile, tile), tile)


def for_steps(steps, body, unroll=False):
    if steps == 1:
        body(0)
    else:
        lax.fori_loop(0, steps, lambda j, c: (body(j), c)[1], 0, unroll=unroll)


def split_halves(core, store):
    for c in range(CORES):

        @pl.when(core == c)
        def _():
            for second in range(2):
                store(second, (c + second) % 2)


def first_partials(where, shard, weights, masks):
    _, rows, feats = shard.shape
    half = rows // 2
    units = weights[0].shape[1]
    blocks = feats // BLOCK
    _, steps, at = tiles(units)

    def body(where_ref, pair, masks_ref, *refs):
        w_refs, (keep_ref, send_ref), bufs = refs[:3], refs[3:5], refs[5:8]
        expanded, lhs, sems = refs[8:11], refs[11], refs[12]
        col, row, core = where_ref[0], where_ref[1], where_ref[2]

        def copies(j):
            part = at(j)
            spots = [(slice(None), part), (slice(None), part), (part, slice(None))]
            return [
                pltpu.make_async_copy(src.at[spot], dst.at[spot], sems.at[k, j])
                for k, (src, dst, spot) in enumerate(zip(w_refs, bufs, spots))
            ]

        def start(j):
            for copy in copies(j):
                copy.start()

        for_steps(steps, start)
        count = masks_ref.shape[1]
        block = lax.div(
            row * units + lax.broadcasted_iota(jnp.int32, (count, units), 1), BLOCK
        )
        pick = (lax.broadcasted_iota(jnp.int32, (count, units), 0) == block).astype(F32)
        pick = pick.astype(BF16)
        total = masks_ref.shape[0] // 3
        feature = col * blocks + lax.broadcasted_iota(jnp.int32, (blocks, total), 0)
        mine = (
            (lax.broadcasted_iota(jnp.int32, (blocks, total), 1) == feature)
            .astype(F32)
            .astype(BF16)
        )
        for k, out in enumerate(expanded):
            mask = masks_ref[pl.ds(k * total, total), :].astype(F32).astype(BF16)
            mask = dot_nn(mine, mask)
            if k < 2:
                out[...] = dot_nn(mask.astype(BF16), pick)
            else:
                out[...] = dot_tn(pick, mask.T.astype(BF16))

        def store(second, side):
            lhs[:, pl.ds(second * half, half), :] = pair[:, pl.ds(side * half, half), :]

        split_halves(core, store)

        def step(j):
            part = at(j)
            for copy in copies(j):
                copy.wait()
            gate = keep_rows(bufs[0][:, part], expanded[0][:, part])
            up = keep_rows(bufs[1][:, part], expanded[1][:, part])
            down = keep_columns(bufs[2][part, :], expanded[2][part, :])
            bufs[0][:, part] = gate
            bufs[1][:, part] = up
            bufs[2][part, :] = down
            for k, out in enumerate((dot_nn(lhs[0], gate), dot_nn(lhs[0], up), dot_nt(lhs[1], down))):
                keep_ref[k, :, part] = out[:half]
                send_ref[k, :, part] = out[half:]

        for_steps(steps, step)

    out_shape = [jax.ShapeDtypeStruct((3, half, units), F32)] * 2
    out_shape += [jax.ShapeDtypeStruct(w.shape, w.dtype) for w in weights]
    out_shape += [jax.ShapeDtypeStruct((blocks, units), F32)] * 2
    out_shape.append(jax.ShapeDtypeStruct((units, blocks), F32))
    return pl.pallas_call(
        body,
        in_specs=[SMEM, VMEM, VMEM] + [HBM] * 3,
        out_specs=[VMEM] * 8,
        out_shape=out_shape,
        scratch_shapes=[
            pltpu.VMEM((2, rows, feats), BF16),
            pltpu.SemaphoreType.DMA((3, steps)),
        ],
        cost_estimate=cost(12 * half * feats * units, shard, *weights, *out_shape),
        compiler_params=params(FIRST_MIB),
        name="first_partials",
    )(where, shard, masks, *weights)


def partials(where, shards, weights, travels):
    n = len(shards)
    _, rows, feats = shards[0].shape
    half = rows // 2
    own = n * half
    units = weights[0].shape[1]
    _, steps, at = tiles(units)

    def body(where_ref, *refs):
        pairs = refs[:n]
        gate_ref, up_ref, down_ref, keep_ref, send_ref, lhs = refs[n:]
        core = where_ref[2]

        def store(second, side):
            for i, pair in enumerate(pairs):
                lhs[:, pl.ds(second * own + i * half, half), :] = pair[
                    :, pl.ds(side * half, half), :
                ]

        split_halves(core, store)

        def step(j):
            part = at(j)
            outs = (
                dot_nn(lhs[0], gate_ref[:, part]),
                dot_nn(lhs[0], up_ref[:, part]),
                dot_nt(lhs[1], down_ref[part, :]),
            )
            for k, out in enumerate(outs):
                keep_ref[k, :, part] = out[:own]
                send_ref[k, :, part] = out[own:].astype(travels)

        for_steps(steps, step, True)

    out_shape = [jax.ShapeDtypeStruct((3, own, units), d) for d in (F32, travels)]
    return pl.pallas_call(
        body,
        in_specs=[SMEM] + [VMEM] * (n + 3),
        out_specs=[VMEM] * 2,
        out_shape=out_shape,
        scratch_shapes=[pltpu.VMEM((2, 2 * own, feats), BF16)],
        cost_estimate=cost(12 * own * feats * units, *shards, *weights, *out_shape),
        compiler_params=params(PARTIALS_MIB),
        name="partials",
    )(where, *shards, *weights)


def finish(where, parts):
    _, rows, feats = parts[0].shape
    half = rows // 2

    def body(where_ref, *refs):
        part_refs, outs = refs[:-2], refs[-2:]
        core = where_ref[2]
        for k, out in enumerate(outs):
            total = part_refs[0][k].astype(F32)
            for ref in part_refs[1:]:
                total = total + ref[k].astype(F32)
            total = total.astype(BF16)
            low, high = total[:half], total[half:]
            out[pl.ds(0, half), :] = jnp.where(core == 1, high, low)
            out[pl.ds(half, half), :] = jnp.where(core == 1, low, high)

    out_shape = [jax.ShapeDtypeStruct((rows, feats), BF16)] * 2
    return pl.pallas_call(
        body,
        in_specs=[SMEM] + [VMEM] * len(parts),
        out_specs=[VMEM] * 2,
        out_shape=out_shape,
        cost_estimate=cost(2 * rows * feats * len(parts), *parts, *out_shape),
        compiler_params=params(8),
        name="finish",
    )(where, *parts)


def activate(keep, near, far):
    def body(*refs):
        keep_ref, near_ref = refs[:2]
        far_refs, out_ref = refs[2:-1], refs[-1]

        def total(k):
            value = keep_ref[k] + near_ref[k].astype(F32)
            for ref in far_refs:
                value = value + ref[k].astype(F32)
            return value

        gate, up, hidden_grad = total(0), total(1), total(2)
        sig = jax.nn.sigmoid(gate)
        act = gate * sig
        out_ref[0] = (act * up).astype(BF16)
        out_ref[1] = (hidden_grad * up * sig * (1.0 + gate * (1.0 - sig))).astype(BF16)
        out_ref[2] = (hidden_grad * act).astype(BF16)

    n = 3 + len(far)
    return pl.pallas_call(
        body,
        in_specs=[VMEM] * (n - 1),
        out_specs=VMEM,
        out_shape=jax.ShapeDtypeStruct(keep.shape, BF16),
        cost_estimate=cost(20 * keep.size, keep, near, *far),
        compiler_params=params(8),
        name="activate",
    )(keep, near, *far)


def products(shards, slots, sizes, weights):
    pieces, spots = [], []
    for own, other, place, half in shards:
        for piece in (own, other):
            known = [k for k, p in enumerate(pieces) if p is piece]
            if not known:
                pieces.append(piece)
            spots.append((known[0] if known else len(pieces) - 1, place * half))
    n = len(pieces)
    units = pieces[0].shape[2]
    feats = weights[0].shape[0]
    tokens = 2 * half * len(shards)
    _, steps, at = tiles(feats)
    outs_n = len(sizes)

    def body(*refs):
        gate_ref, up_ref, down_ref = refs[n : n + 3]
        outs, lhs = refs[n + 3 : n + 3 + outs_n], refs[n + 3 + outs_n]
        for k, (piece, row) in enumerate(spots):
            lhs[:, pl.ds(k * half, half), :] = refs[piece][:, pl.ds(row, half), :]

        def step(j):
            part = at(j)
            sums = (
                dot_nn(lhs[0], down_ref[:, part]),
                dot_nt(lhs[1], gate_ref[part, :]) + dot_nt(lhs[2], up_ref[part, :]),
            )
            for i, (out, place) in enumerate(slots):
                for k in range(2):
                    outs[out][place, k, :, part] = sums[k][
                        2 * half * i : 2 * half * (i + 1)
                    ].astype(outs[out].dtype)

        for_steps(steps, step, True)

    out_shape = [
        jax.ShapeDtypeStruct((size, 2, 2 * half, feats), BF16 if k else F32)
        for k, size in enumerate(sizes)
    ]
    return pl.pallas_call(
        body,
        in_specs=[VMEM] * (n + 3),
        out_specs=[VMEM] * outs_n,
        out_shape=out_shape,
        scratch_shapes=[pltpu.VMEM((3, tokens, units), BF16)],
        cost_estimate=cost(6 * tokens * feats * units, *pieces, *weights, *out_shape),
        compiler_params=params(PRODUCTS_MIB),
        name="products",
    )(*pieces, *weights)


def gather_rows(where, groups):
    shards = [s for g in groups for s in g]
    _, rows, feats = shards[0].shape
    half = rows // 2
    tokens = len(shards) * rows

    def body(where_ref, *refs):
        pairs, (turned, rhs), lhs = refs[:-3], refs[-3:-1], refs[-1]

        def store(second, side):
            row, shard = 0, 0
            for group in groups:
                size = len(group) * half
                for i in range(len(group)):
                    at_row = pl.ds(row + second * size + i * half, half)
                    lhs[at_row, :] = pairs[shard + i][0, pl.ds(side * half, half), :]
                    rhs[at_row, :] = pairs[shard + i][1, pl.ds(side * half, half), :]
                row += 2 * size
                shard += len(group)

        split_halves(where_ref[2], store)
        turned[...] = lhs[...].T

    out_shape = [
        jax.ShapeDtypeStruct((feats, tokens), BF16),
        jax.ShapeDtypeStruct((tokens, feats), BF16),
    ]
    return pl.pallas_call(
        body,
        in_specs=[SMEM] + [VMEM] * len(shards),
        out_specs=[VMEM] * 2,
        out_shape=out_shape,
        scratch_shapes=[pltpu.VMEM((tokens, feats), BF16)],
        cost_estimate=cost(0, *shards, *out_shape),
        compiler_params=params(8),
        name="gather_rows",
    )(where, *shards)


def weight_grads(turned, rhs, parts, keeps):
    pieces = [a for pair in parts for a in pair]
    m = len(pieces)
    feats, tokens = turned.shape
    units = pieces[0].shape[2]
    tile, steps, at = tiles(units)

    def body(turned_ref, rhs_ref, *refs):
        piece_refs = refs[:m]
        kg, ku, kd = refs[m : m + 3]
        grads = refs[m + 3 : m + 6]
        gate_buf, up_buf, down_buf, sems = refs[m + 6 :]

        def copies(j):
            part = at(j)
            return [
                pltpu.make_async_copy(src.at[j], dst, sems.at[k, j])
                for k, (src, dst) in enumerate(
                    (
                        (gate_buf, grads[0].at[:, part]),
                        (up_buf, grads[1].at[:, part]),
                        (down_buf, grads[2].at[part, :]),
                    )
                )
            ]

        def step(j):
            part = at(j)
            pre = [
                jnp.concatenate([p[k, :, part] for p in piece_refs], axis=0) for k in range(3)
            ]
            gate_copy, up_copy, down_copy = copies(j)
            gate_buf[j] = keep_rows(dot_nn(turned_ref[...], pre[1]), kg[:, part])
            gate_copy.start()
            up_buf[j] = keep_rows(dot_nn(turned_ref[...], pre[2]), ku[:, part])
            up_copy.start()
            down_buf[j] = keep_columns(dot_tn(pre[0], rhs_ref[...]), kd[part, :])
            down_copy.start()

        def finish(j):
            for copy in copies(j):
                copy.wait()

        for_steps(steps, step)
        for_steps(steps, finish)

    out_shape = [
        jax.ShapeDtypeStruct((feats, units), F32),
        jax.ShapeDtypeStruct((feats, units), F32),
        jax.ShapeDtypeStruct((units, feats), F32),
    ]
    return pl.pallas_call(
        body,
        in_specs=[VMEM] * (m + 5),
        out_specs=[HBM] * 3,
        out_shape=out_shape,
        scratch_shapes=[
            pltpu.VMEM((steps, feats, tile), F32),
            pltpu.VMEM((steps, feats, tile), F32),
            pltpu.VMEM((steps, tile, feats), F32),
            pltpu.SemaphoreType.DMA((3, steps)),
        ],
        cost_estimate=cost(6 * tokens * feats * units, turned, rhs, *pieces, *out_shape),
        compiler_params=params(32),
        name="weight_grads",
    )(turned, rhs, *pieces, *keeps)


def per_device(
    rows_n,
    cols_n,
    tokens,
    gate_weight,
    up_weight,
    down_weight,
    gate_mask,
    up_mask,
    down_mask,
    out_grad,
):
    cores = CORES if cols_n % CORES == 0 else 1
    ys = cols_n // cores
    xs = 1
    while (2 * xs) ** 2 <= rows_n and rows_n % (2 * xs) == 0:
        xs *= 2
    zs = rows_n // xs
    row_index = lax.axis_index("row")
    col_index = lax.axis_index("col")
    core = col_index % cores

    def shift_z(value, by):
        pairs = [(i, ((i // xs + by) % zs) * xs + i % xs) for i in range(rows_n)]
        return lax.ppermute(value, "row", pairs)

    def shift_x(value, by):
        pairs = [(i, i // xs * xs + (i % xs + by) % xs) for i in range(rows_n)]
        return lax.ppermute(value, "row", pairs)

    def shift_y(value, by):
        pairs = [(i, (i // cores + by) % ys * cores + i % cores) for i in range(cols_n)]
        return lax.ppermute(value, "col", pairs)

    def swap_core(value):
        pairs = [(i, i // cores * cores + (i % cores + 1) % cores) for i in range(cols_n)]
        return lax.ppermute(value, "col", pairs)

    where = jnp.stack([col_index, row_index, core])
    pair = jnp.stack([tokens, out_grad])
    masks = jnp.concatenate([gate_mask, up_mask, down_mask.T])

    far_z = [d for k in range(1, zs // 2 + 1) for d in dict.fromkeys((k, zs - k))]
    held = {(0, 0): pair}
    for k, dz in enumerate(far_z):
        held[dz, 0] = shift_z(pair, dz)
    for dx in range(1, xs):
        held[0, dx] = shift_x(pair, dx)
    for k, dz in enumerate(far_z):
        for dx in range(1, xs):
            held[dz, dx] = shift_x(held[dz, 0], dx)

    far_x = range(1, xs)
    near_z = far_z[:2]
    chunks = {"own": [(0, 0)], "a": [(dz, 0) for dz in near_z]}
    chunks["b"] = [(dz, dx) for dz in near_z[:1] for dx in far_x]
    for k in range(2, len(far_z), 2):
        chunks[f"m{k}"] = [(dz, dx) for dx in range(xs) for dz in far_z[k : k + 2]]
    chunks["c"] = [(dz, dx) for dz in near_z[1:] for dx in far_x]
    chunks["x"] = [(0, dx) for dx in far_x]
    groups = {"b": near_z[:1]}
    for k in range(2, len(far_z), 2):
        groups[f"m{k}"] = far_z[k : k + 2]
    groups["c"] = near_z[1:]
    groups["x"] = [0]
    chunks = {name: chunk for name, chunk in chunks.items() if chunk}
    groups = {name: group for name, group in groups.items() if group}

    parts = {}
    weights = (gate_weight, up_weight, down_weight)
    for name, chunk in chunks.items():
        shards = [held[s] for s in chunk]
        if name == "own":
            keep, send, *rest = first_partials(where, *shards, weights, masks)
            weights, keeps = rest[:3], rest[3:]
        else:
            keep, send = partials(where, shards, weights, BF16 if name == "a" else F32)
        near = swap_core(send)
        out = (keep + near).astype(BF16)
        far = [shift_y(out, by) for by in range(1, ys)]
        own = activate(keep, near, far)
        parts[name] = (own, swap_core(own))

    half = tokens.shape[0] // 2
    homes = {
        s: (*parts[name], k, half) for name, chunk in chunks.items() for k, s in enumerate(chunk)
    }
    terms = []
    for group in groups.values():
        shards = [(dz, dx) for dx in range(xs) for dz in group]
        outs = products(
            [homes[s] for s in shards],
            [(dx, group.index(dz)) for dz, dx in shards],
            [len(group)] * xs,
            weights,
        )
        sums = [outs[0]]
        for dx in far_x:
            sums.append(shift_x(outs[dx], -dx))
        for k, dz in enumerate(group):
            if not dz:
                terms.extend(value[k] for value in sums[::-1])
                continue
            value = sum(value[k].astype(F32) for value in sums)
            terms.append(shift_z(value.astype(BF16), -dz))
    turned, rhs = gather_rows(where, [[held[s] for s in chunk] for chunk in chunks.values()])
    grads = weight_grads(turned, rhs, [parts[name] for name in chunks], keeps)
    return (*finish(where, terms[::-1]), *grads)


def solution(mesh):
    def whole(*args):
        return per_device(mesh.shape["row"], mesh.shape["col"], *args)

    return jax.shard_map(
        whole,
        mesh=mesh,
        in_specs=(
            P("row", "col"),
            P("col", "row"),
            P("col", "row"),
            P("row", "col"),
            P(),
            P(),
            P(),
            P("row", "col"),
        ),
        out_specs=(
            P("row", "col"),
            P("row", "col"),
            P("col", "row"),
            P("col", "row"),
            P("row", "col"),
        ),
        check_vma=False,
    )
```

```python
import jax
import jax.numpy as jnp
from jax import lax
from jax.experimental import pallas as pl
from jax.experimental.pallas import tpu as pltpu
from jax.sharding import PartitionSpec as P

BLOCK = 128
CORES = 2
BF16 = jnp.bfloat16
F32 = jnp.float32
MIB = 1 << 20
FIRST_MIB = 39
PARTIALS_MIB = 8
PRODUCTS_MIB = 10
HBM = pl.BlockSpec(memory_space=pltpu.HBM)
VMEM = pl.BlockSpec(memory_space=pltpu.VMEM)
SMEM = pl.BlockSpec(memory_space=pltpu.SMEM)


def tile_of(units):
    return 256 if units % 256 == 0 else units


def keep_rows(weight, mask):
    mask = mask.astype(weight.dtype)
    parts = [
        weight[k * BLOCK : (k + 1) * BLOCK] * mask[k : k + 1] for k in range(mask.shape[0])
    ]
    return jnp.concatenate(parts, axis=0)


def keep_columns(weight, mask):
    parts = []
    for k in range(mask.shape[1]):
        wide = jnp.broadcast_to(mask[:, k : k + 1], (mask.shape[0], BLOCK))
        parts.append(weight[:, k * BLOCK : (k + 1) * BLOCK] * wide.astype(weight.dtype))
    return jnp.concatenate(parts, axis=1)


def dot_nn(left, right):
    return jnp.dot(left, right, preferred_element_type=F32)


def dot_nt(left, right):
    return lax.dot_general(
        left, right, (((1,), (1,)), ((), ())), preferred_element_type=F32
    )


def dot_tn(left, right):
    return lax.dot_general(
        left, right, (((0,), (0,)), ((), ())), preferred_element_type=F32
    )


def cost(flops, *arrays):
    return pl.CostEstimate(
        flops=flops,
        bytes_accessed=sum(a.size * a.dtype.itemsize for a in arrays),
        transcendentals=0,
    )


def params(mib):
    return pltpu.CompilerParams(vmem_limit_bytes=mib * MIB)


def tiles(units):
    tile = tile_of(units)
    return tile, units // tile, lambda j: pl.ds(pl.multiple_of(j * tile, tile), tile)


def for_steps(steps, body, unroll=False):
    if steps == 1:
        body(0)
    else:
        lax.fori_loop(0, steps, lambda j, c: (body(j), c)[1], 0, unroll=unroll)


def split_halves(core, store):
    for c in range(CORES):

        @pl.when(core == c)
        def _():
            for second in range(2):
                store(second, (c + second) % 2)


def first_partials(where, shard, weights, masks):
    _, rows, feats = shard.shape
    half = rows // 2
    units = weights[0].shape[1]
    blocks = feats // BLOCK
    _, steps, at = tiles(units)

    def body(where_ref, pair, masks_ref, *refs):
        w_refs, (keep_ref, send_ref), bufs = refs[:3], refs[3:5], refs[5:8]
        expanded, lhs, sems = refs[8:11], refs[11], refs[12]
        col, row, core = where_ref[0], where_ref[1], where_ref[2]

        def copies(j):
            part = at(j)
            spots = [(slice(None), part), (slice(None), part), (part, slice(None))]
            return [
                pltpu.make_async_copy(src.at[spot], dst.at[spot], sems.at[k, j])
                for k, (src, dst, spot) in enumerate(zip(w_refs, bufs, spots))
            ]

        def start(j):
            for copy in copies(j):
                copy.start()

        for_steps(steps, start)
        count = masks_ref.shape[1]
        block = lax.div(
            row * units + lax.broadcasted_iota(jnp.int32, (count, units), 1), BLOCK
        )
        pick = (lax.broadcasted_iota(jnp.int32, (count, units), 0) == block).astype(F32)
        pick = pick.astype(BF16)
        total = masks_ref.shape[0] // 3
        feature = col * blocks + lax.broadcasted_iota(jnp.int32, (blocks, total), 0)
        mine = (
            (lax.broadcasted_iota(jnp.int32, (blocks, total), 1) == feature)
            .astype(F32)
            .astype(BF16)
        )
        for k, out in enumerate(expanded):
            mask = masks_ref[pl.ds(k * total, total), :].astype(F32).astype(BF16)
            mask = dot_nn(mine, mask)
            if k < 2:
                out[...] = dot_nn(mask.astype(BF16), pick)
            else:
                out[...] = dot_tn(pick, mask.T.astype(BF16))

        def store(second, side):
            lhs[:, pl.ds(second * half, half), :] = pair[:, pl.ds(side * half, half), :]

        split_halves(core, store)

        def step(j):
            part = at(j)
            for copy in copies(j):
                copy.wait()
            gate = keep_rows(bufs[0][:, part], expanded[0][:, part])
            up = keep_rows(bufs[1][:, part], expanded[1][:, part])
            down = keep_columns(bufs[2][part, :], expanded[2][part, :])
            bufs[0][:, part] = gate
            bufs[1][:, part] = up
            bufs[2][part, :] = down
            for k, out in enumerate((dot_nn(lhs[0], gate), dot_nn(lhs[0], up), dot_nt(lhs[1], down))):
                keep_ref[k, :, part] = out[:half]
                send_ref[k, :, part] = out[half:]

        for_steps(steps, step)

    out_shape = [jax.ShapeDtypeStruct((3, half, units), F32)] * 2
    out_shape += [jax.ShapeDtypeStruct(w.shape, w.dtype) for w in weights]
    out_shape += [jax.ShapeDtypeStruct((blocks, units), F32)] * 2
    out_shape.append(jax.ShapeDtypeStruct((units, blocks), F32))
    return pl.pallas_call(
        body,
        in_specs=[SMEM, VMEM, VMEM] + [HBM] * 3,
        out_specs=[VMEM] * 8,
        out_shape=out_shape,
        scratch_shapes=[
            pltpu.VMEM((2, rows, feats), BF16),
            pltpu.SemaphoreType.DMA((3, steps)),
        ],
        cost_estimate=cost(12 * half * feats * units, shard, *weights, *out_shape),
        compiler_params=params(FIRST_MIB),
        name="first_partials",
    )(where, shard, masks, *weights)


def partials(where, shards, weights, travels):
    n = len(shards)
    _, rows, feats = shards[0].shape
    half = rows // 2
    own = n * half
    units = weights[0].shape[1]
    _, steps, at = tiles(units)

    def body(where_ref, *refs):
        pairs = refs[:n]
        gate_ref, up_ref, down_ref, keep_ref, send_ref, lhs = refs[n:]
        core = where_ref[2]

        def store(second, side):
            for i, pair in enumerate(pairs):
                lhs[:, pl.ds(second * own + i * half, half), :] = pair[
                    :, pl.ds(side * half, half), :
                ]

        split_halves(core, store)

        def step(j):
            part = at(j)
            outs = (
                dot_nn(lhs[0], gate_ref[:, part]),
                dot_nn(lhs[0], up_ref[:, part]),
                dot_nt(lhs[1], down_ref[part, :]),
            )
            for k, out in enumerate(outs):
                keep_ref[k, :, part] = out[:own]
                send_ref[k, :, part] = out[own:].astype(travels)

        for_steps(steps, step, True)

    out_shape = [jax.ShapeDtypeStruct((3, own, units), d) for d in (F32, travels)]
    return pl.pallas_call(
        body,
        in_specs=[SMEM] + [VMEM] * (n + 3),
        out_specs=[VMEM] * 2,
        out_shape=out_shape,
        scratch_shapes=[pltpu.VMEM((2, 2 * own, feats), BF16)],
        cost_estimate=cost(12 * own * feats * units, *shards, *weights, *out_shape),
        compiler_params=params(PARTIALS_MIB),
        name="partials",
    )(where, *shards, *weights)


def finish(where, parts):
    _, rows, feats = parts[0].shape
    half = rows // 2

    def body(where_ref, *refs):
        part_refs, outs = refs[:-2], refs[-2:]
        core = where_ref[2]
        for k, out in enumerate(outs):
            total = part_refs[0][k].astype(F32)
            for ref in part_refs[1:]:
                total = total + ref[k].astype(F32)
            total = total.astype(BF16)
            low, high = total[:half], total[half:]
            out[pl.ds(0, half), :] = jnp.where(core == 1, high, low)
            out[pl.ds(half, half), :] = jnp.where(core == 1, low, high)

    out_shape = [jax.ShapeDtypeStruct((rows, feats), BF16)] * 2
    return pl.pallas_call(
        body,
        in_specs=[SMEM] + [VMEM] * len(parts),
        out_specs=[VMEM] * 2,
        out_shape=out_shape,
        cost_estimate=cost(2 * rows * feats * len(parts), *parts, *out_shape),
        compiler_params=params(8),
        name="finish",
    )(where, *parts)


def activate(keep, near, far):
    def body(*refs):
        keep_ref, near_ref = refs[:2]
        far_refs, out_ref = refs[2:-1], refs[-1]

        def total(k):
            value = keep_ref[k] + near_ref[k].astype(F32)
            for ref in far_refs:
                value = value + ref[k].astype(F32)
            return value

        gate, up, hidden_grad = total(0), total(1), total(2)
        sig = jax.nn.sigmoid(gate)
        act = gate * sig
        out_ref[0] = (act * up).astype(BF16)
        out_ref[1] = (hidden_grad * up * sig * (1.0 + gate * (1.0 - sig))).astype(BF16)
        out_ref[2] = (hidden_grad * act).astype(BF16)

    n = 3 + len(far)
    return pl.pallas_call(
        body,
        in_specs=[VMEM] * (n - 1),
        out_specs=VMEM,
        out_shape=jax.ShapeDtypeStruct(keep.shape, BF16),
        cost_estimate=cost(20 * keep.size, keep, near, *far),
        compiler_params=params(8),
        name="activate",
    )(keep, near, *far)


def products(shards, slots, sizes, weights):
    pieces, spots = [], []
    for own, other, place, half in shards:
        for piece in (own, other):
            known = [k for k, p in enumerate(pieces) if p is piece]
            if not known:
                pieces.append(piece)
            spots.append((known[0] if known else len(pieces) - 1, place * half))
    n = len(pieces)
    units = pieces[0].shape[2]
    feats = weights[0].shape[0]
    tokens = 2 * half * len(shards)
    _, steps, at = tiles(feats)
    outs_n = len(sizes)

    def body(*refs):
        gate_ref, up_ref, down_ref = refs[n : n + 3]
        outs, lhs = refs[n + 3 : n + 3 + outs_n], refs[n + 3 + outs_n]
        for k, (piece, row) in enumerate(spots):
            lhs[:, pl.ds(k * half, half), :] = refs[piece][:, pl.ds(row, half), :]

        def step(j):
            part = at(j)
            sums = (
                dot_nn(lhs[0], down_ref[:, part]),
                dot_nt(lhs[1], gate_ref[part, :]) + dot_nt(lhs[2], up_ref[part, :]),
            )
            for i, (out, place) in enumerate(slots):
                for k in range(2):
                    outs[out][place, k, :, part] = sums[k][
                        2 * half * i : 2 * half * (i + 1)
                    ].astype(outs[out].dtype)

        for_steps(steps, step, True)

    out_shape = [
        jax.ShapeDtypeStruct((size, 2, 2 * half, feats), BF16 if k else F32)
        for k, size in enumerate(sizes)
    ]
    return pl.pallas_call(
        body,
        in_specs=[VMEM] * (n + 3),
        out_specs=[VMEM] * outs_n,
        out_shape=out_shape,
        scratch_shapes=[pltpu.VMEM((3, tokens, units), BF16)],
        cost_estimate=cost(6 * tokens * feats * units, *pieces, *weights, *out_shape),
        compiler_params=params(PRODUCTS_MIB),
        name="products",
    )(*pieces, *weights)


def gather_rows(where, groups):
    shards = [s for g in groups for s in g]
    _, rows, feats = shards[0].shape
    half = rows // 2
    tokens = len(shards) * rows

    def body(where_ref, *refs):
        pairs, (turned, rhs), lhs = refs[:-3], refs[-3:-1], refs[-1]

        def store(second, side):
            row, shard = 0, 0
            for group in groups:
                size = len(group) * half
                for i in range(len(group)):
                    at_row = pl.ds(row + second * size + i * half, half)
                    lhs[at_row, :] = pairs[shard + i][0, pl.ds(side * half, half), :]
                    rhs[at_row, :] = pairs[shard + i][1, pl.ds(side * half, half), :]
                row += 2 * size
                shard += len(group)

        split_halves(where_ref[2], store)
        turned[...] = lhs[...].T

    out_shape = [
        jax.ShapeDtypeStruct((feats, tokens), BF16),
        jax.ShapeDtypeStruct((tokens, feats), BF16),
    ]
    return pl.pallas_call(
        body,
        in_specs=[SMEM] + [VMEM] * len(shards),
        out_specs=[VMEM] * 2,
        out_shape=out_shape,
        scratch_shapes=[pltpu.VMEM((tokens, feats), BF16)],
        cost_estimate=cost(0, *shards, *out_shape),
        compiler_params=params(8),
        name="gather_rows",
    )(where, *shards)


def weight_grads(turned, rhs, parts, keeps):
    pieces = [a for pair in parts for a in pair]
    m = len(pieces)
    feats, tokens = turned.shape
    units = pieces[0].shape[2]
    tile, steps, at = tiles(units)

    def body(turned_ref, rhs_ref, *refs):
        piece_refs = refs[:m]
        kg, ku, kd = refs[m : m + 3]
        grads = refs[m + 3 : m + 6]
        gate_buf, up_buf, down_buf, sems = refs[m + 6 :]

        def copies(j):
            part = at(j)
            return [
                pltpu.make_async_copy(src.at[j], dst, sems.at[k, j])
                for k, (src, dst) in enumerate(
                    (
                        (gate_buf, grads[0].at[:, part]),
                        (up_buf, grads[1].at[:, part]),
                        (down_buf, grads[2].at[part, :]),
                    )
                )
            ]

        def step(j):
            part = at(j)
            pre = [
                jnp.concatenate([p[k, :, part] for p in piece_refs], axis=0) for k in range(3)
            ]
            gate_copy, up_copy, down_copy = copies(j)
            gate_buf[j] = keep_rows(dot_nn(turned_ref[...], pre[1]), kg[:, part])
            gate_copy.start()
            up_buf[j] = keep_rows(dot_nn(turned_ref[...], pre[2]), ku[:, part])
            up_copy.start()
            down_buf[j] = keep_columns(dot_tn(pre[0], rhs_ref[...]), kd[part, :])
            down_copy.start()

        def finish(j):
            for copy in copies(j):
                copy.wait()

        for_steps(steps, step)
        for_steps(steps, finish)

    out_shape = [
        jax.ShapeDtypeStruct((feats, units), F32),
        jax.ShapeDtypeStruct((feats, units), F32),
        jax.ShapeDtypeStruct((units, feats), F32),
    ]
    return pl.pallas_call(
        body,
        in_specs=[VMEM] * (m + 5),
        out_specs=[HBM] * 3,
        out_shape=out_shape,
        scratch_shapes=[
            pltpu.VMEM((steps, feats, tile), F32),
            pltpu.VMEM((steps, feats, tile), F32),
            pltpu.VMEM((steps, tile, feats), F32),
            pltpu.SemaphoreType.DMA((3, steps)),
        ],
        cost_estimate=cost(6 * tokens * feats * units, turned, rhs, *pieces, *out_shape),
        compiler_params=params(32),
        name="weight_grads",
    )(turned, rhs, *pieces, *keeps)


def per_device(
    rows_n,
    cols_n,
    tokens,
    gate_weight,
    up_weight,
    down_weight,
    gate_mask,
    up_mask,
    down_mask,
    out_grad,
):
    cores = CORES if cols_n % CORES == 0 else 1
    ys = cols_n // cores
    xs = 1
    while (2 * xs) ** 2 <= rows_n and rows_n % (2 * xs) == 0:
        xs *= 2
    zs = rows_n // xs
    row_index = lax.axis_index("row")
    col_index = lax.axis_index("col")
    core = col_index % cores

    def shift_z(value, by):
        pairs = [(i, ((i // xs + by) % zs) * xs + i % xs) for i in range(rows_n)]
        return lax.ppermute(value, "row", pairs)

    def shift_x(value, by):
        pairs = [(i, i // xs * xs + (i % xs + by) % xs) for i in range(rows_n)]
        return lax.ppermute(value, "row", pairs)

    def shift_y(value, by):
        pairs = [(i, (i // cores + by) % ys * cores + i % cores) for i in range(cols_n)]
        return lax.ppermute(value, "col", pairs)

    def swap_core(value):
        pairs = [(i, i // cores * cores + (i % cores + 1) % cores) for i in range(cols_n)]
        return lax.ppermute(value, "col", pairs)

    where = jnp.stack([col_index, row_index, core])
    pair = jnp.stack([tokens, out_grad])
    masks = jnp.concatenate([gate_mask, up_mask, down_mask.T])

    far_z = [d for k in range(1, zs // 2 + 1) for d in dict.fromkeys((k, zs - k))]
    held = {(0, 0): pair}
    for k, dz in enumerate(far_z):
        held[dz, 0] = shift_z(pair, dz)
    for dx in range(1, xs):
        held[0, dx] = shift_x(pair, dx)
    for k, dz in enumerate(far_z):
        for dx in range(1, xs):
            held[dz, dx] = shift_x(held[dz, 0], dx)

    far_x = range(1, xs)
    near_z = far_z[:2]
    chunks = {"own": [(0, 0)], "a": [(dz, 0) for dz in near_z]}
    chunks["b"] = [(dz, dx) for dz in near_z[:1] for dx in far_x]
    for k in range(2, len(far_z), 2):
        chunks[f"m{k}"] = [(dz, dx) for dx in range(xs) for dz in far_z[k : k + 2]]
    chunks["c"] = [(dz, dx) for dz in near_z[1:] for dx in far_x]
    chunks["x"] = [(0, dx) for dx in far_x]
    groups = {"b": near_z[:1]}
    for k in range(2, len(far_z), 2):
        groups[f"m{k}"] = far_z[k : k + 2]
    groups["c"] = near_z[1:]
    groups["x"] = [0]
    chunks = {name: chunk for name, chunk in chunks.items() if chunk}
    groups = {name: group for name, group in groups.items() if group}

    parts = {}
    weights = (gate_weight, up_weight, down_weight)
    for name, chunk in chunks.items():
        shards = [held[s] for s in chunk]
        if name == "own":
            keep, send, *rest = first_partials(where, *shards, weights, masks)
            weights, keeps = rest[:3], rest[3:]
        else:
            keep, send = partials(where, shards, weights, BF16 if name == "a" else F32)
        near = swap_core(send)
        out = (keep + near).astype(BF16)
        far = [shift_y(out, by) for by in range(1, ys)]
        own = activate(keep, near, far)
        parts[name] = (own, swap_core(own))

    half = tokens.shape[0] // 2
    homes = {
        s: (*parts[name], k, half) for name, chunk in chunks.items() for k, s in enumerate(chunk)
    }
    terms, relayed = [], None
    for group in groups.values():
        shards = [(dz, dx) for dx in range(xs) for dz in group]
        outs = products(
            [homes[s] for s in shards],
            [(dx, group.index(dz)) for dz, dx in shards],
            [len(group)] * xs,
            weights,
        )
        sums = [outs[0]]
        for dx in far_x:
            sums.append(shift_x(outs[dx], -dx))
        for k, dz in enumerate(group):
            if not dz:
                terms.extend(value[k] for value in sums[::-1])
                continue
            value = sum(value[k].astype(F32) for value in sums)
            if dz == zs - 1 and relayed is not None:
                value = value + relayed
                relayed = None
            if zs == 4 and dz == 2:
                relayed = shift_z(value.astype(BF16), 1)
                continue
            terms.append(shift_z(value.astype(BF16), -dz))
    turned, rhs = gather_rows(where, [[held[s] for s in chunk] for chunk in chunks.values()])
    grads = weight_grads(turned, rhs, [parts[name] for name in chunks], keeps)
    return (*finish(where, terms[::-1]), *grads)


def solution(mesh):
    def whole(*args):
        return per_device(mesh.shape["row"], mesh.shape["col"], *args)

    return jax.shard_map(
        whole,
        mesh=mesh,
        in_specs=(
            P("row", "col"),
            P("col", "row"),
            P("col", "row"),
            P("row", "col"),
            P(),
            P(),
            P(),
            P("row", "col"),
        ),
        out_specs=(
            P("row", "col"),
            P("row", "col"),
            P("col", "row"),
            P("col", "row"),
            P("row", "col"),
        ),
        check_vma=False,
    )
```
